1024 devices in a mesh: seq: 64 (over z, y_lo, core), chan: 16 (over y_hi, x).
Axes of the slice: x: 4, y: 8 (y_hi: 4, y_lo: 2; y = y_hi * 2 + y_lo), z: 16, core: 2. Of those that a mesh axis runs over, the one named last changes fastest.
Arguments:
- values: bfloat16 [16384, 4096], P('seq', 'chan'), may hold values from -6 to 6
- gate_in: bfloat16 [16384, 4096], P('seq', 'chan'), may hold values from -6 to 6
- gate_out: bfloat16 [16384, 4096], P('seq', 'chan'), may hold values from -6 to 6
- spectrum: float32 [2, 16, 1024, 4096], P(None, None, 'seq', 'chan'), may hold values from -6 to 6
- out_weight: bfloat16 [4096, 8192], P('chan'), may hold values from -0.125 to 0.125
Outputs:
- mixed: bfloat16 [16384, 8192], P('seq', 'chan')
The draws below stay inside these ranges and needn't reach their ends.
All inputs are finite; a program needn't handle non-finite values.
Results may differ from the reference program's by a relative error of at most 0.024.
Values may be sent and summed in bfloat16 or wider, within the bound.
A program may use at most 64 MiB of HBM per device.

```python
import math
import jax
import jax.numpy as jnp
from jax import lax

DIM = 8192
CHANNELS = 4096
BLOCK = 1024
TOKENS = 16384
SPAN = 16
N_CHAN = 16


def raised(values, stream_key, source, target, blocks, factor):
    owner, partner = [(jnp.arange(values.shape[dim]) // (values.shape[dim] // blocks)).reshape([-1 if axis == dim else 1 for axis in range(values.ndim)]) for dim in (source, target)]
    chosen = jax.random.permutation(stream_key, blocks)[partner]
    strong = (owner == chosen) | (owner == (partner + blocks // 2) % blocks)
    return jnp.where(strong, factor * values, values)


def level_of(key, shape, cuts, low, top_value):
    gain = 1.0
    for position, parts in cuts:
        draws = jax.random.uniform(jax.random.fold_in(jax.random.fold_in(key, 6), position), (parts,), jnp.float32, low / len(cuts), top_value / len(cuts))
        gain = gain * jnp.repeat(jnp.exp(draws), shape[position] // parts).reshape((-1,) + (1,) * (len(shape) - 1 - position))
    return gain


def scatter_about(rng, dims, deviation, limit, split=(), kind=jnp.bfloat16):
    loudness = level_of(rng, dims, split, -0.22, 0.18) if split else 1.0
    values = jax.random.normal(rng, dims, jnp.float32) * deviation * loudness
    return jnp.minimum(jnp.maximum(values, -limit), limit).astype(kind)


def bell_draw_with(stream_key, extent, spread, bound, shards, heavy, kind=jnp.bfloat16):
    entries = spread * jax.random.normal(stream_key, extent, jnp.float32)
    if shards:
        entries = entries * level_of(stream_key, extent, shards, -0.22, 0.18)
    return jnp.clip(raised(entries, jax.random.fold_in(stream_key, 3), *heavy), -bound, bound).astype(kind)


def setup_inputs(seed: int = 0) -> dict:
    splits = jax.random.split(jax.random.key(seed), 6)
    return {
        "values": scatter_about(splits[0], (TOKENS, CHANNELS), 1.0, 6.0, ((0, 64), (1, 16))),
        "gate_in": scatter_about(splits[1], (TOKENS, CHANNELS), 1.0, 6.0, ((0, 64), (1, 16))),
        "gate_out": scatter_about(splits[2], (TOKENS, CHANNELS), 1.0, 6.0, ((0, 64), (1, 16))),
        "spectrum": scatter_about(splits[3], (2, SPAN, BLOCK, CHANNELS), 1.0, 6.0, ((2, 64), (3, 16)), jnp.float32),
        "out_weight": bell_draw_with(splits[4], (CHANNELS, DIM), CHANNELS ** -0.5, 0.125, ((0, 16),), (0, 1, 16, 2.0)),
    }


def angle_table(first, second, period):
    product = (first[:, None] * second[None, :]) % period
    return product.astype(jnp.float32) * (2.0 * math.pi / period)


def settle(array):
    return lax.optimization_barrier(array.astype(jnp.bfloat16)).astype(jnp.float32)


def reference(values, gate_in, gate_out, spectrum, out_weight):
    span = TOKENS // BLOCK
    full_block = jnp.arange(BLOCK, dtype=jnp.int32)
    full_span = jnp.arange(span, dtype=jnp.int32)
    block_angle = angle_table(full_block, full_block, BLOCK)
    block_cos = jnp.cos(block_angle).astype(jnp.bfloat16).astype(jnp.float32)
    block_sin = jnp.sin(block_angle).astype(jnp.bfloat16).astype(jnp.float32)
    span_angle = angle_table(full_span, full_span, span)
    span_cos = jnp.cos(span_angle).astype(jnp.bfloat16).astype(jnp.float32)
    span_sin = jnp.sin(span_angle).astype(jnp.bfloat16).astype(jnp.float32)
    source = settle(values.astype(jnp.float32) * gate_in.astype(jnp.float32))
    grid = source.reshape(BLOCK, span, CHANNELS)
    cos_part = jnp.einsum('ac,abh->bch', block_cos, grid)
    sin_part = jnp.einsum('ac,abh->bch', block_sin, grid)
    turn = angle_table(full_span, full_block, TOKENS)
    turn_cos = jnp.cos(turn)[:, :, None]
    turn_sin = jnp.sin(turn)[:, :, None]
    twist_re = cos_part * turn_cos - sin_part * turn_sin
    twist_im = -sin_part * turn_cos - cos_part * turn_sin
    twisted = settle(jnp.stack([twist_re, twist_im]))
    with_cos = jnp.einsum('bd,kbch->kdch', span_cos, twisted)
    with_sin = jnp.einsum('bd,kbch->kdch', span_sin, twisted)
    freq_re = with_cos[0] + with_sin[1]
    freq_im = with_cos[1] - with_sin[0]
    prod_re = freq_re * spectrum[0] - freq_im * spectrum[1]
    prod_im = freq_re * spectrum[1] + freq_im * spectrum[0]
    product = settle(jnp.stack([prod_re, prod_im]))
    back_cos = jnp.einsum('db,kdch->kcbh', span_cos, product)
    back_sin = jnp.einsum('db,kdch->kcbh', span_sin, product)
    back_re = (back_cos[0] - back_sin[1]) / span
    back_im = (back_cos[1] + back_sin[0]) / span
    turn_back = jnp.transpose(turn)
    back_tc = jnp.cos(turn_back)[:, :, None]
    back_ts = jnp.sin(turn_back)[:, :, None]
    rotated_re = settle(back_re * back_tc - back_im * back_ts)
    rotated_im = settle(back_im * back_tc + back_re * back_ts)
    conv = (jnp.einsum('ac,cbh->abh', block_cos, rotated_re) - jnp.einsum('ac,cbh->abh', block_sin, rotated_im)) / BLOCK
    conv = settle(conv.reshape(TOKENS, CHANNELS))
    gated = (conv * gate_out.astype(jnp.float32)).astype(jnp.bfloat16)
    width = CHANNELS // N_CHAN
    total = jnp.zeros((TOKENS, DIM), jnp.float32)
    for group in range(N_CHAN):
        partial_sum = jnp.dot(gated[:, group * width:(group + 1) * width], out_weight[group * width:(group + 1) * width], preferred_element_type=jnp.float32)
        total = total + settle(partial_sum)
    return total.astype(jnp.bfloat16)
```

```python
import functools
import math

import jax
import jax.numpy as jnp
import ml_dtypes
import numpy as np
from jax import lax
from jax.experimental import pallas as pl
from jax.experimental.pallas import tpu as pltpu
from jax.sharding import PartitionSpec as P

BLOCK = 1024
SPAN = 16
TOKENS = 16384
SEQ = 64
HALF = 8
LANES = 128
OWN = 4
MESH = pl.DeviceIdType.MESH
BF16 = jnp.bfloat16
F32 = jnp.float32


def tables():
    freq = np.arange(BLOCK)
    base = (16 * np.arange(SEQ)[:, None] + np.arange(HALF)[None, :]).reshape(-1)
    angle = 2.0 * math.pi * ((freq[:, None] * base[None, :]) % BLOCK) / BLOCK
    forward = np.concatenate([np.cos(angle), -np.sin(angle)]).astype(ml_dtypes.bfloat16)
    inverse = np.ascontiguousarray(forward.T)
    lane = np.arange(LANES)
    place = lane % SPAN + 128 * (lane // 64)
    turn = 2.0 * math.pi * ((freq[:, None] * place[None, :]) % TOKENS) / TOKENS
    twist = np.stack([np.cos(turn), -np.sin(turn)]).astype(np.float32)
    span = np.arange(SPAN)
    span_angle = 2.0 * math.pi * ((span[:, None] * span[None, :]) % SPAN) / SPAN
    cos, sin = np.cos(span_angle), np.sin(span_angle)
    same = np.eye(OWN)

    def spread(block):
        return np.kron(same, block)

    re_rows = [np.tile(spread(cos), (2, 1)), np.tile(spread(sin), (2, 1))]
    im_rows = [np.tile(-spread(sin), (2, 1)), np.tile(spread(cos), (2, 1))]
    re, im = np.concatenate(re_rows), np.concatenate(im_rows)
    mix = np.concatenate([re, re, -im, im], axis=1).astype(ml_dtypes.bfloat16)
    back_re = np.concatenate([spread(cos.T), -spread(sin.T)])
    back_im = np.concatenate([spread(sin.T), spread(cos.T)])
    unmix = np.concatenate([back_re, back_re, back_im, back_im], axis=1)
    unmix = (unmix.astype(ml_dtypes.bfloat16).astype(np.float32) / TOKENS).astype(ml_dtypes.bfloat16)
    chan = np.arange(SEQ * OWN)
    pick = (chan[None, :] // OWN == np.arange(SEQ)[:, None]).astype(ml_dtypes.bfloat16)
    pick_t = np.ascontiguousarray(pick.T)
    row = np.arange(2 * SPAN)
    fold = (row[:, None] // SPAN == lane[None, :] // 64) & (row[:, None] % SPAN == lane[None, :] % SPAN)
    fold = fold.astype(ml_dtypes.bfloat16)
    return forward, inverse, twist, mix, unmix, pick, pick_t, fold


def dot(left, right):
    return jnp.dot(left, right, preferred_element_type=F32)


def dot_t(left, right):
    return lax.dot_general(left, right, (((1,), (1,)), ((), ())), preferred_element_type=F32)


def conv_kernel(
    values_h, gate_in_h, gate_out_h, spectrum_h, forward_h, inverse_h, twist_h,
    mix_h, unmix_h, pick_h, pick_t_h, fold_h, out,
    values, gate_in, gate_out, spectrum, forward, inverse, twist, mix, unmix, pick, pick_t, fold,
    stage, tok_send, tok_recv, wide, spec_send, spec_recv, freq, turned, back_send, back_recv,
    load_sem, send_sem, recv_sem,
):
    me = lax.axis_index("seq")
    sources = (values_h, gate_in_h, pick_h, forward_h, twist_h, mix_h, unmix_h, inverse_h,
               gate_out_h, pick_t_h, fold_h)
    targets = (values, gate_in, pick, forward, twist, mix, unmix, inverse,
               gate_out, pick_t, fold)
    loads = [
        pltpu.make_async_copy(src, dst, load_sem.at[i]) for i, (src, dst) in enumerate(zip(sources, targets))
    ]
    halves = [
        pltpu.make_async_copy(
            spectrum_h.at[:, pl.ds(LANES * i, LANES)], spectrum.at[i], load_sem.at[len(loads) + i]
        )
        for i in range(2)
    ]
    for load in loads[:3] + halves + loads[3:]:
        load.start()
    barrier = pltpu.get_barrier_semaphore()

    @pl.loop(1, SEQ)
    def _(i):
        pl.semaphore_signal(
            barrier, inc=1, device_id={"seq": lax.rem(me + i, SEQ)}, device_id_type=MESH
        )

    def exchange(send, recv, slot):
        @pl.loop(1, SEQ)
        def _(i):
            peer = lax.rem(me + i, SEQ)
            pltpu.make_async_remote_copy(
                src_ref=send.at[peer], dst_ref=recv.at[me],
                send_sem=send_sem.at[slot], recv_sem=recv_sem.at[slot],
                device_id={"seq": peer}, device_id_type=MESH,
            ).start()

    def settled(ref, sem):
        part = ref.at[pl.ds(0, SEQ - 1)]
        pltpu.make_async_copy(part, part, sem).wait()

    lane = lax.broadcasted_iota(jnp.int32, (SPAN, SEQ * OWN), 1)
    masks = [lax.rem(lane, OWN) == h for h in range(OWN)]
    for load in loads[:3]:
        load.wait()
    picked = pick[...]
    for low in range(HALF):
        pieces = []
        for high in range(2):
            rows = pl.ds((high * HALF + low) * SPAN, SPAN)
            block = (values[rows, :].astype(F32) * gate_in[rows, :].astype(F32)).astype(BF16).astype(F32)
            pieces += [jnp.where(mask, block, 0.0) for mask in masks]
        spread = jnp.concatenate(pieces, axis=0).astype(BF16)
        stage[pl.ds(low, SEQ, stride=HALF), :] = dot_t(picked, spread)
    tok_send[...] = stage[...].reshape(SEQ, HALF, LANES).astype(BF16)
    pl.semaphore_wait(barrier, SEQ - 1)
    exchange(tok_send, tok_recv, 0)
    tok_recv[me] = tok_send[me]
    for load in halves:
        load.wait()
    for col in range(SPAN):
        rows = pl.ds(col, 2 * SPAN, stride=SPAN)
        block = jnp.concatenate([spectrum[0, rows, :], spectrum[1, rows, :]], axis=1)
        pieces = []
        for part in range(2):
            half = block[part * SPAN:(part + 1) * SPAN]
            pieces += [jnp.where(mask, half, 0.0) for mask in masks]
        spread = jnp.concatenate(pieces, axis=0).astype(BF16)
        wide[pl.ds(col, SEQ, stride=SPAN), :] = dot_t(picked, spread)
    spec_send[...] = wide[...].reshape(SEQ, SPAN, LANES).astype(BF16)
    exchange(spec_send, spec_recv, 1)
    spec_recv[me] = spec_send[me]
    for load in loads[3:]:
        load.wait()
    settled(tok_recv, recv_sem.at[0])
    columns = tok_recv[...].reshape(SEQ * HALF, LANES)
    step = 256

    @pl.loop(0, BLOCK // step)
    def _(i):
        rows = pl.ds(pl.multiple_of(i * step, step), step)
        im_rows = pl.ds(pl.multiple_of(BLOCK + i * step, step), step)
        re, im = dot(forward[rows, :], columns), dot(forward[im_rows, :], columns)
        tr, ti = twist[0, rows, :], twist[1, rows, :]
        pair = jnp.concatenate([re * tr - im * ti, re * ti + im * tr], axis=1).astype(BF16)
        freq[rows, :] = dot(pair, mix[...])

    settled(spec_recv, recv_sem.at[1])

    @pl.loop(0, BLOCK // step)
    def _(i):
        rows = pl.ds(pl.multiple_of(i * step, step), step)
        im_rows = pl.ds(pl.multiple_of(BLOCK + i * step, step), step)
        filt = spec_recv[pl.ds(i * (step // SPAN), step // SPAN)].reshape(step, LANES).astype(F32)
        prod = freq[rows, :LANES] * filt + freq[rows, LANES:] * pltpu.roll(filt, 64, 1)
        back = dot(prod.astype(BF16), unmix[...])
        re, im = back[:, :LANES], back[:, LANES:]
        tr, ti = twist[0, rows, :], twist[1, rows, :]
        turned[rows, :] = (re * tr + im * ti).astype(BF16)
        turned[im_rows, :] = (im * tr - re * ti).astype(BF16)

    @pl.loop(0, 4)
    def _(i):
        rows = pl.ds(pl.multiple_of(i * 128, 128), 128)
        conv = dot(inverse[rows, :], turned[...])
        back_send[pl.ds(i * 16, 16)] = conv.reshape(16, HALF, LANES).astype(BF16)

    exchange(back_send, back_recv, 2)
    back_recv[me] = back_send[me]
    settled(back_recv, recv_sem.at[2])
    stage[...] = back_recv[...].reshape(SEQ * HALF, LANES).astype(F32)
    chan_row = lax.rem(lax.broadcasted_iota(jnp.int32, (SEQ * OWN, LANES), 0), OWN)
    chan_lane = lax.rem(lax.broadcasted_iota(jnp.int32, (SEQ * OWN, LANES), 1) // SPAN, OWN)
    for low in range(HALF):
        block = stage[pl.ds(low, SEQ, stride=HALF), :].astype(BF16)
        spread = jnp.where(chan_row == chan_lane, dot(pick_t[...], block), 0.0).astype(BF16)
        conv = dot_t(fold[...], spread)
        for high in range(2):
            rows = pl.ds((high * HALF + low) * SPAN, SPAN)
            gate = gate_out[rows, :].astype(F32)
            out[rows, :] = (conv[high * SPAN:(high + 1) * SPAN] * gate).astype(BF16)
    settled(tok_send, send_sem.at[0])
    settled(spec_send, send_sem.at[1])
    settled(back_send, send_sem.at[2])


def convolve(values, gate_in, gate_out, spectrum):
    forward, inverse, twist, mix, unmix, pick, pick_t, fold = tables()
    rows, width = values.shape
    flat = spectrum.reshape(2 * SPAN * SPAN, width)
    loaded = [(values.shape, BF16)] * 3 + [((2, 2 * SPAN * SPAN, LANES), F32)]
    loaded += [(t.shape, F32 if t.dtype == np.float32 else BF16) for t in
               (forward, inverse, twist, mix, unmix, pick, pick_t, fold)]
    scratch = [pltpu.VMEM(shape, dtype) for shape, dtype in loaded]
    scratch += [
        pltpu.VMEM((SEQ * HALF, LANES), F32),
        pltpu.VMEM((SEQ, HALF, LANES), BF16),
        pltpu.VMEM((SEQ, HALF, LANES), BF16),
        pltpu.VMEM((SEQ * SPAN, LANES), F32),
        pltpu.VMEM((SEQ, SPAN, LANES), BF16),
        pltpu.VMEM((SEQ, SPAN, LANES), BF16),
        pltpu.VMEM((BLOCK, 2 * LANES), F32),
        pltpu.VMEM((2 * BLOCK, LANES), BF16),
        pltpu.VMEM((SEQ, HALF, LANES), BF16),
        pltpu.VMEM((SEQ, HALF, LANES), BF16),
        pltpu.SemaphoreType.DMA((len(loaded) + 1,)),
        pltpu.SemaphoreType.DMA((3,)),
        pltpu.SemaphoreType.DMA((3,)),
    ]
    return pl.pallas_call(
        conv_kernel,
        out_shape=jax.ShapeDtypeStruct((rows, width), BF16),
        in_specs=[pl.BlockSpec(memory_space=pl.ANY)] * 12,
        out_specs=pl.BlockSpec(memory_space=pltpu.VMEM),
        scratch_shapes=scratch,
        compiler_params=pltpu.CompilerParams(
            collective_id=0, has_side_effects=True, vmem_limit_bytes=40 << 20
        ),
        name="convolve",
    )(values, gate_in, gate_out, flat, *[jnp.asarray(t) for t in
      (forward, inverse, twist, mix, unmix, pick, pick_t, fold)])


def shards(values, gate_in, gate_out, spectrum, out_weight):
    gated = convolve(values, gate_in, gate_out, spectrum)
    partial_sum = jnp.dot(gated, out_weight, preferred_element_type=F32)
    return lax.psum_scatter(partial_sum.astype(BF16), "chan", scatter_dimension=1, tiled=True)


def solution(mesh):
    placed = (
        P("seq", "chan"),
        P("seq", "chan"),
        P("seq", "chan"),
        P(None, None, "seq", "chan"),
        P("chan", None),
    )
    return jax.shard_map(
        shards, mesh=mesh, in_specs=placed, out_specs=P("seq", "chan"), check_vma=False
    )
```

```python
import functools
import math

import jax
import jax.numpy as jnp
import ml_dtypes
import numpy as np
from jax import lax
from jax.experimental import pallas as pl
from jax.experimental.pallas import tpu as pltpu
from jax.sharding import PartitionSpec as P

BLOCK = 1024
SPAN = 16
TOKENS = 16384
SEQ = 64
HALF = 8
LANES = 128
SIDE = 4
OWN = 4
MESH = pl.DeviceIdType.MESH
BF16 = jnp.bfloat16
F32 = jnp.float32


def tables():
    freq = np.arange(BLOCK)
    base = (16 * np.arange(SEQ)[:, None] + np.arange(HALF)[None, :]).reshape(-1)
    angle = 2.0 * math.pi * ((freq[:, None] * base[None, :]) % BLOCK) / BLOCK
    forward = np.concatenate([np.cos(angle), -np.sin(angle)]).astype(ml_dtypes.bfloat16)
    inverse = np.ascontiguousarray(forward.T)
    lane = np.arange(LANES)
    place = lane % SPAN + 128 * (lane // 64)
    turn = 2.0 * math.pi * ((freq[:, None] * place[None, :]) % TOKENS) / TOKENS
    twist = np.stack([np.cos(turn), -np.sin(turn)]).astype(np.float32)
    span = np.arange(SPAN)
    span_angle = 2.0 * math.pi * ((span[:, None] * span[None, :]) % SPAN) / SPAN
    cos, sin = np.cos(span_angle), np.sin(span_angle)
    same = np.eye(OWN)

    def spread(block):
        return np.kron(same, block)

    re_rows = [np.tile(spread(cos), (2, 1)), np.tile(spread(sin), (2, 1))]
    im_rows = [np.tile(-spread(sin), (2, 1)), np.tile(spread(cos), (2, 1))]
    re, im = np.concatenate(re_rows), np.concatenate(im_rows)
    mix = np.concatenate([re, re, -im, im], axis=1).astype(ml_dtypes.bfloat16)
    back_re = np.concatenate([spread(cos.T), -spread(sin.T)])
    back_im = np.concatenate([spread(sin.T), spread(cos.T)])
    unmix = np.concatenate([back_re, back_re, back_im, back_im], axis=1)
    unmix = (unmix.astype(ml_dtypes.bfloat16).astype(np.float32) / TOKENS).astype(ml_dtypes.bfloat16)
    chan = np.arange(SEQ * OWN)
    pick = (chan[None, :] // OWN == np.arange(SEQ)[:, None]).astype(ml_dtypes.bfloat16)
    pick_t = np.ascontiguousarray(pick.T)
    row = np.arange(2 * SPAN)
    fold = (row[:, None] // SPAN == lane[None, :] // 64) & (row[:, None] % SPAN == lane[None, :] % SPAN)
    fold = fold.astype(ml_dtypes.bfloat16)
    return forward, inverse, twist, mix, unmix, pick, pick_t, fold


def dot(left, right):
    return jnp.dot(left, right, preferred_element_type=F32)


def dot_t(left, right):
    return lax.dot_general(left, right, (((1,), (1,)), ((), ())), preferred_element_type=F32)


def layer_kernel(
    values_h, gate_in_h, gate_out_h, spectrum_h, weight_h, forward_h, inverse_h, twist_h,
    mix_h, unmix_h, pick_h, pick_t_h, fold_h, out,
    values, gate_in, gate_out, spectrum, forward, inverse, twist, mix, unmix, pick, pick_t, fold,
    stage, tok_send, tok_recv, wide, spec_send, spec_recv, freq, turned, back_send, back_recv,
    weight, gated, total, part_send, part_recv,
    load_sem, send_sem, recv_sem, weight_sem, pair_sem, gated_sem, part_sem,
):
    me = lax.axis_index("seq")
    group = lax.axis_index("chan")
    col_x, col_y = lax.rem(group, SIDE), group // SIDE
    core = lax.rem(me, 2)
    sibling = me + 1 - 2 * core
    sources = (values_h, gate_in_h, pick_h, forward_h, twist_h, mix_h, unmix_h, inverse_h,
               gate_out_h, pick_t_h, fold_h)
    targets = (values, gate_in, pick, forward, twist, mix, unmix, inverse,
               gate_out, pick_t, fold)
    loads = [
        pltpu.make_async_copy(src, dst, load_sem.at[i]) for i, (src, dst) in enumerate(zip(sources, targets))
    ]
    halves = [
        pltpu.make_async_copy(
            spectrum_h.at[:, pl.ds(LANES * i, LANES)], spectrum.at[i], load_sem.at[len(loads) + i]
        )
        for i in range(2)
    ]
    for load in loads[:3] + halves + loads[3:]:
        load.start()
    half_k, cols_each = weight.shape[1] // (2 * SIDE), weight.shape[2]

    def own_weight(i):
        cols = pl.multiple_of((i * SIDE + col_x) * cols_each, cols_each)
        rows = pl.multiple_of(col_x * 2 * half_k, 2 * half_k)
        return pltpu.make_async_copy(
            weight_h.at[:, pl.ds(cols, cols_each)], weight.at[i, pl.ds(rows, 2 * half_k), :],
            load_sem.at[len(loads) + 2 + i],
        )

    for i in range(SIDE):
        own_weight(i).start()
    barrier = pltpu.get_barrier_semaphore()

    @pl.loop(1, SEQ)
    def _(i):
        pl.semaphore_signal(
            barrier, inc=1, device_id={"seq": lax.rem(me + i, SEQ)}, device_id_type=MESH
        )

    def at_x(i):
        return col_y * SIDE + lax.rem(col_x + i, SIDE)

    def at_y(i):
        return lax.rem(col_y + i, SIDE) * SIDE + col_x

    for i in range(1, SIDE):
        for peer in (at_x(i), at_y(i)):
            pl.semaphore_signal(barrier, inc=1, device_id={"chan": peer}, device_id_type=MESH)

    def exchange(send, recv, slot):
        @pl.loop(1, SEQ)
        def _(i):
            peer = lax.rem(me + i, SEQ)
            pltpu.make_async_remote_copy(
                src_ref=send.at[peer], dst_ref=recv.at[me],
                send_sem=send_sem.at[slot], recv_sem=recv_sem.at[slot],
                device_id={"seq": peer}, device_id_type=MESH,
            ).start()

    def settled(ref, sem):
        part = ref.at[pl.ds(0, SEQ - 1)]
        pltpu.make_async_copy(part, part, sem).wait()

    lane = lax.broadcasted_iota(jnp.int32, (SPAN, SEQ * OWN), 1)
    masks = [lax.rem(lane, OWN) == h for h in range(OWN)]
    for load in loads[:3]:
        load.wait()
    picked = pick[...]
    for low in range(HALF):
        pieces = []
        for high in range(2):
            rows = pl.ds((high * HALF + low) * SPAN, SPAN)
            block = (values[rows, :].astype(F32) * gate_in[rows, :].astype(F32)).astype(BF16).astype(F32)
            pieces += [jnp.where(mask, block, 0.0) for mask in masks]
        spread = jnp.concatenate(pieces, axis=0).astype(BF16)
        stage[pl.ds(low, SEQ, stride=HALF), :] = dot_t(picked, spread)
    tok_send[...] = stage[...].reshape(SEQ, HALF, LANES).astype(BF16)
    pl.semaphore_wait(barrier, SEQ - 1 + 2 * (SIDE - 1))
    exchange(tok_send, tok_recv, 0)
    tok_recv[me] = tok_send[me]
    half_rows = pl.multiple_of(core * half_k, half_k)

    @pl.loop(0, SIDE)
    def _(i):
        for j in range(1, SIDE):
            cols = pl.multiple_of((i * SIDE + lax.rem(col_x + j, SIDE)) * cols_each, cols_each)
            rows = pl.multiple_of(col_x * 2 * half_k + half_rows, half_k)
            pltpu.make_async_remote_copy(
                src_ref=weight_h.at[pl.ds(half_rows, half_k), pl.ds(cols, cols_each)],
                dst_ref=weight.at[i, pl.ds(rows, half_k), :],
                send_sem=weight_sem.at[SIDE], recv_sem=weight_sem.at[col_x],
                device_id={"chan": at_x(j)}, device_id_type=MESH,
            ).start()
    for load in halves:
        load.wait()
    for col in range(SPAN):
        rows = pl.ds(col, 2 * SPAN, stride=SPAN)
        block = jnp.concatenate([spectrum[0, rows, :], spectrum[1, rows, :]], axis=1)
        pieces = []
        for part in range(2):
            half = block[part * SPAN:(part + 1) * SPAN]
            pieces += [jnp.where(mask, half, 0.0) for mask in masks]
        spread = jnp.concatenate(pieces, axis=0).astype(BF16)
        wide[pl.ds(col, SEQ, stride=SPAN), :] = dot_t(picked, spread)
    spec_send[...] = wide[...].reshape(SEQ, SPAN, LANES).astype(BF16)
    exchange(spec_send, spec_recv, 1)
    spec_recv[me] = spec_send[me]
    for load in loads[3:]:
        load.wait()
    settled(tok_recv, recv_sem.at[0])
    columns = tok_recv[...].reshape(SEQ * HALF, LANES)
    step = 256

    @pl.loop(0, BLOCK // step)
    def _(i):
        rows = pl.ds(pl.multiple_of(i * step, step), step)
        im_rows = pl.ds(pl.multiple_of(BLOCK + i * step, step), step)
        re, im = dot(forward[rows, :], columns), dot(forward[im_rows, :], columns)
        tr, ti = twist[0, rows, :], twist[1, rows, :]
        pair = jnp.concatenate([re * tr - im * ti, re * ti + im * tr], axis=1).astype(BF16)
        freq[rows, :] = dot(pair, mix[...])

    settled(spec_recv, recv_sem.at[1])

    @pl.loop(0, BLOCK // step)
    def _(i):
        rows = pl.ds(pl.multiple_of(i * step, step), step)
        im_rows = pl.ds(pl.multiple_of(BLOCK + i * step, step), step)
        filt = spec_recv[pl.ds(i * (step // SPAN), step // SPAN)].reshape(step, LANES).astype(F32)
        prod = freq[rows, :LANES] * filt + freq[rows, LANES:] * pltpu.roll(filt, 64, 1)
        back = dot(prod.astype(BF16), unmix[...])
        re, im = back[:, :LANES], back[:, LANES:]
        tr, ti = twist[0, rows, :], twist[1, rows, :]
        turned[rows, :] = (re * tr + im * ti).astype(BF16)
        turned[im_rows, :] = (im * tr - re * ti).astype(BF16)

    @pl.loop(0, 4)
    def _(i):
        rows = pl.ds(pl.multiple_of(i * 128, 128), 128)
        conv = dot(inverse[rows, :], turned[...])
        back_send[pl.ds(i * 16, 16)] = conv.reshape(16, HALF, LANES).astype(BF16)

    exchange(back_send, back_recv, 2)
    back_recv[me] = back_send[me]

    def weight_half(source, which):
        rows = pl.multiple_of(source * 2 * half_k + which * half_k, half_k)
        return weight.at[:, pl.ds(rows, half_k), :]

    for i in (1, 3, 2):
        source = lax.rem(col_x + i, SIDE)
        mine = weight_half(source, core)
        pltpu.make_async_copy(mine, mine, weight_sem.at[source]).wait()
        pltpu.make_async_remote_copy(
            src_ref=mine, dst_ref=mine, send_sem=pair_sem.at[SIDE], recv_sem=pair_sem.at[source],
            device_id={"seq": sibling}, device_id_type=MESH,
        ).start()

    settled(back_recv, recv_sem.at[2])
    stage[...] = back_recv[...].reshape(SEQ * HALF, LANES).astype(F32)
    chan_row = lax.rem(lax.broadcasted_iota(jnp.int32, (SEQ * OWN, LANES), 0), OWN)
    chan_lane = lax.rem(lax.broadcasted_iota(jnp.int32, (SEQ * OWN, LANES), 1) // SPAN, OWN)
    width = SEQ * OWN
    own_cols = pl.ds(pl.multiple_of(col_x * width, width), width)
    for low in range(HALF):
        block = stage[pl.ds(low, SEQ, stride=HALF), :].astype(BF16)
        spread = jnp.where(chan_row == chan_lane, dot(pick_t[...], block), 0.0).astype(BF16)
        conv = dot_t(fold[...], spread)
        for high in range(2):
            rows = pl.ds((high * HALF + low) * SPAN, SPAN)
            gate = gate_out[rows, :].astype(F32)
            gated[rows, own_cols] = (conv[high * SPAN:(high + 1) * SPAN] * gate).astype(BF16)
    for i in (2, 1, 3):
        pltpu.make_async_remote_copy(
            src_ref=gated.at[:, own_cols], dst_ref=gated.at[:, own_cols],
            send_sem=gated_sem.at[SIDE], recv_sem=gated_sem.at[col_x],
            device_id={"chan": at_x(i)}, device_id_type=MESH,
        ).start()
    for i in range(SIDE):
        own_weight(i).wait()
    for i in (1, 3, 2):
        source = lax.rem(col_x + i, SIDE)
        other = weight_half(source, 1 - core)
        pltpu.make_async_copy(other, other, pair_sem.at[source]).wait()
    for i in (1, 3, 2):
        source = lax.rem(col_x + i, SIDE)
        cols = gated.at[:, pl.ds(pl.multiple_of(source * width, width), width)]
        pltpu.make_async_copy(cols, cols, gated_sem.at[source]).wait()
    for i in (2, 1, 3, 0):
        target = lax.rem(col_y + i, SIDE)
        for half in range(2):
            cols = pl.ds(half * cols_each // 2, cols_each // 2)
            part = dot(gated[...], weight[target, :, cols])
            if i:
                part_send[target, :, cols] = part.astype(BF16)
            else:
                total[:, cols] = part
        if i:
            pltpu.make_async_remote_copy(
                src_ref=part_send.at[target], dst_ref=part_recv.at[col_y],
                send_sem=part_sem.at[SIDE], recv_sem=part_sem.at[col_y],
                device_id={"chan": at_y(i)}, device_id_type=MESH,
            ).start()
    for i in (1, 3, 2):
        source = lax.rem(col_y + i, SIDE)
        pltpu.make_async_copy(part_recv.at[source], part_recv.at[source], part_sem.at[source]).wait()
        total[...] += part_recv[source].astype(F32)
    out[...] = total[...].astype(BF16)
    settled(tok_send, send_sem.at[0])
    settled(spec_send, send_sem.at[1])
    settled(back_send, send_sem.at[2])
    three = weight.at[:, pl.ds(0, 3 * half_k), :]
    pltpu.make_async_copy(three, three, weight_sem.at[SIDE]).wait()
    pltpu.make_async_copy(three, three, pair_sem.at[SIDE]).wait()
    sent = gated.at[:, pl.ds(0, 3 * width)]
    pltpu.make_async_copy(sent, sent, gated_sem.at[SIDE]).wait()
    sent = part_send.at[pl.ds(0, 3)]
    pltpu.make_async_copy(sent, sent, part_sem.at[SIDE]).wait()


def layer(values, gate_in, gate_out, spectrum, out_weight):
    forward, inverse, twist, mix, unmix, pick, pick_t, fold = tables()
    rows, width = values.shape
    cols_each = out_weight.shape[1] // (SIDE * SIDE)
    flat = spectrum.reshape(2 * SPAN * SPAN, width)
    loaded = [(values.shape, BF16)] * 3 + [((2, 2 * SPAN * SPAN, LANES), F32)]
    loaded += [(t.shape, F32 if t.dtype == np.float32 else BF16) for t in
               (forward, inverse, twist, mix, unmix, pick, pick_t, fold)]
    scratch = [pltpu.VMEM(shape, dtype) for shape, dtype in loaded]
    scratch += [
        pltpu.VMEM((SEQ * HALF, LANES), F32),
        pltpu.VMEM((SEQ, HALF, LANES), BF16),
        pltpu.VMEM((SEQ, HALF, LANES), BF16),
        pltpu.VMEM((SEQ * SPAN, LANES), F32),
        pltpu.VMEM((SEQ, SPAN, LANES), BF16),
        pltpu.VMEM((SEQ, SPAN, LANES), BF16),
        pltpu.VMEM((BLOCK, 2 * LANES), F32),
        pltpu.VMEM((2 * BLOCK, LANES), BF16),
        pltpu.VMEM((SEQ, HALF, LANES), BF16),
        pltpu.VMEM((SEQ, HALF, LANES), BF16),
        pltpu.VMEM((SIDE, SIDE * width, cols_each), BF16),
        pltpu.VMEM((rows, SIDE * width), BF16),
        pltpu.VMEM((rows, cols_each), F32),
        pltpu.VMEM((SIDE, rows, cols_each), BF16),
        pltpu.VMEM((SIDE, rows, cols_each), BF16),
        pltpu.SemaphoreType.DMA((len(loaded) + 1 + SIDE,)),
        pltpu.SemaphoreType.DMA((3,)),
        pltpu.SemaphoreType.DMA((3,)),
        pltpu.SemaphoreType.DMA((SIDE + 1,)),
        pltpu.SemaphoreType.DMA((SIDE + 1,)),
        pltpu.SemaphoreType.DMA((SIDE + 1,)),
        pltpu.SemaphoreType.DMA((SIDE + 1,)),
    ]
    return pl.pallas_call(
        layer_kernel,
        out_shape=jax.ShapeDtypeStruct((rows, cols_each), BF16),
        in_specs=[pl.BlockSpec(memory_space=pltpu.HBM)] * 13,
        out_specs=pl.BlockSpec(memory_space=pltpu.VMEM),
        scratch_shapes=scratch,
        compiler_params=pltpu.CompilerParams(
            collective_id=0, has_side_effects=True, vmem_limit_bytes=60 << 20
        ),
        name="layer",
    )(values, gate_in, gate_out, flat, out_weight, *[jnp.asarray(t) for t in
      (forward, inverse, twist, mix, unmix, pick, pick_t, fold)])


def solution(mesh):
    placed = (
        P("seq", "chan"),
        P("seq", "chan"),
        P("seq", "chan"),
        P(None, None, "seq", "chan"),
        P("chan", None),
    )
    return jax.shard_map(
        layer, mesh=mesh, in_specs=placed, out_specs=P("seq", "chan"), check_vma=False
    )
```

```python
import functools
import math

import jax
import jax.numpy as jnp
import ml_dtypes
import numpy as np
from jax import lax
from jax.experimental import pallas as pl
from jax.experimental.pallas import tpu as pltpu
from jax.sharding import PartitionSpec as P

BLOCK = 1024
SPAN = 16
TOKENS = 16384
SEQ = 64
HALF = 8
LANES = 128
SIDE = 4
OWN = 4
FAR, DIRECT, MERGED = range(3)
MESH = pl.DeviceIdType.MESH
BF16 = jnp.bfloat16
F32 = jnp.float32


def tables():
    freq = np.arange(BLOCK)
    base = (16 * np.arange(SEQ)[:, None] + np.arange(HALF)[None, :]).reshape(-1)
    angle = 2.0 * math.pi * ((freq[:, None] * base[None, :]) % BLOCK) / BLOCK
    forward = np.concatenate([np.cos(angle), -np.sin(angle)]).astype(ml_dtypes.bfloat16)
    inverse = np.ascontiguousarray(forward.T)
    lane = np.arange(LANES)
    place = lane % SPAN + 128 * (lane // 64)
    turn = 2.0 * math.pi * ((freq[:, None] * place[None, :]) % TOKENS) / TOKENS
    twist = np.stack([np.cos(turn), -np.sin(turn)]).astype(np.float32)
    span = np.arange(SPAN)
    span_angle = 2.0 * math.pi * ((span[:, None] * span[None, :]) % SPAN) / SPAN
    cos, sin = np.cos(span_angle), np.sin(span_angle)
    same = np.eye(OWN)

    def spread(block):
        return np.kron(same, block)

    re_rows = [np.tile(spread(cos), (2, 1)), np.tile(spread(sin), (2, 1))]
    im_rows = [np.tile(-spread(sin), (2, 1)), np.tile(spread(cos), (2, 1))]
    re, im = np.concatenate(re_rows), np.concatenate(im_rows)
    mix = np.concatenate([re, re, -im, im], axis=1).astype(ml_dtypes.bfloat16)
    back_re = np.concatenate([spread(cos.T), -spread(sin.T)])
    back_im = np.concatenate([spread(sin.T), spread(cos.T)])
    unmix = np.concatenate([back_re, back_re, back_im, back_im], axis=1)
    unmix = (unmix.astype(ml_dtypes.bfloat16).astype(np.float32) / TOKENS).astype(ml_dtypes.bfloat16)
    chan = np.arange(SEQ * OWN)
    pick = (chan[None, :] // OWN == np.arange(SEQ)[:, None]).astype(ml_dtypes.bfloat16)
    pick_t = np.ascontiguousarray(pick.T)
    row = np.arange(2 * SPAN)
    fold = (row[:, None] // SPAN == lane[None, :] // 64) & (row[:, None] % SPAN == lane[None, :] % SPAN)
    fold = fold.astype(ml_dtypes.bfloat16)
    return forward, inverse, twist, mix, unmix, pick, pick_t, fold


def dot(left, right):
    return jnp.dot(left, right, preferred_element_type=F32)


def dot_t(left, right):
    return lax.dot_general(left, right, (((1,), (1,)), ((), ())), preferred_element_type=F32)


def layer_kernel(
    values_h, gate_in_h, gate_out_h, spectrum_h, weight_h, forward_h, inverse_h, twist_h,
    mix_h, unmix_h, pick_h, pick_t_h, fold_h, out,
    values, gate_in, gate_out, spectrum, forward, inverse, twist, mix, unmix, pick, pick_t, fold,
    stage, tok_send, tok_recv, wide, spec_send, spec_recv, freq, turned, back_send, back_recv,
    weight, gated, total, kept, part_send, part_recv,
    load_sem, send_sem, recv_sem, weight_sem, pair_sem, gated_sem, part_sem,
):
    me = lax.axis_index("seq")
    group = lax.axis_index("chan")
    col_x, col_y = lax.rem(group, SIDE), group // SIDE
    core = lax.rem(me, 2)
    sibling = me + 1 - 2 * core
    sources = (values_h, gate_in_h, pick_h, forward_h, twist_h, mix_h, unmix_h, inverse_h,
               gate_out_h, pick_t_h, fold_h)
    targets = (values, gate_in, pick, forward, twist, mix, unmix, inverse,
               gate_out, pick_t, fold)
    loads = [
        pltpu.make_async_copy(src, dst, load_sem.at[i]) for i, (src, dst) in enumerate(zip(sources, targets))
    ]
    halves = [
        pltpu.make_async_copy(
            spectrum_h.at[:, pl.ds(LANES * i, LANES)], spectrum.at[i], load_sem.at[len(loads) + i]
        )
        for i in range(2)
    ]
    for load in loads[:3] + halves + loads[3:]:
        load.start()
    half_k, cols_each = weight.shape[1] // (2 * SIDE), weight.shape[2]

    def own_weight(i):
        cols = pl.multiple_of((i * SIDE + col_x) * cols_each, cols_each)
        rows = pl.multiple_of(col_x * 2 * half_k, 2 * half_k)
        return pltpu.make_async_copy(
            weight_h.at[:, pl.ds(cols, cols_each)], weight.at[i, pl.ds(rows, 2 * half_k), :],
            load_sem.at[len(loads) + 2 + i],
        )

    for i in range(SIDE):
        own_weight(i).start()
    barrier = pltpu.get_barrier_semaphore()

    @pl.loop(1, SEQ)
    def _(i):
        pl.semaphore_signal(
            barrier, inc=1, device_id={"seq": lax.rem(me + i, SEQ)}, device_id_type=MESH
        )

    def at_x(i):
        return col_y * SIDE + lax.rem(col_x + i, SIDE)

    def at_y(i):
        return lax.rem(col_y + i, SIDE) * SIDE + col_x

    for i in range(1, SIDE):
        for peer in (at_x(i), at_y(i)):
            pl.semaphore_signal(barrier, inc=1, device_id={"chan": peer}, device_id_type=MESH)

    def exchange(send, recv, slot):
        @pl.loop(0, SEQ - 1)
        def _(i):
            away = SEQ // 2 + ((i + 1) // 2) * (1 - 2 * lax.rem(i, 2))
            peer = lax.rem(me + away, SEQ)
            pltpu.make_async_remote_copy(
                src_ref=send.at[peer], dst_ref=recv.at[me],
                send_sem=send_sem.at[slot], recv_sem=recv_sem.at[slot],
                device_id={"seq": peer}, device_id_type=MESH,
            ).start()

    def settled(ref, sem):
        part = ref.at[pl.ds(0, SEQ - 1)]
        pltpu.make_async_copy(part, part, sem).wait()

    lane = lax.broadcasted_iota(jnp.int32, (SPAN, SEQ * OWN), 1)
    masks = [lax.rem(lane, OWN) == h for h in range(OWN)]
    for load in loads[:3]:
        load.wait()
    picked = pick[...]
    for low in range(HALF):
        pieces = []
        for high in range(2):
            rows = pl.ds((high * HALF + low) * SPAN, SPAN)
            block = (values[rows, :].astype(F32) * gate_in[rows, :].astype(F32)).astype(BF16).astype(F32)
            pieces += [jnp.where(mask, block, 0.0) for mask in masks]
        spread = jnp.concatenate(pieces, axis=0).astype(BF16)
        stage[pl.ds(low, SEQ, stride=HALF), :] = dot_t(picked, spread)
    tok_send[...] = stage[...].reshape(SEQ, HALF, LANES).astype(BF16)
    pl.semaphore_wait(barrier, SEQ - 1 + 2 * (SIDE - 1))
    exchange(tok_send, tok_recv, 0)
    tok_recv[me] = tok_send[me]
    half_rows = pl.multiple_of(core * half_k, half_k)

    @pl.loop(0, SIDE)
    def _(i):
        for j in range(1, SIDE):
            cols = pl.multiple_of((i * SIDE + lax.rem(col_x + j, SIDE)) * cols_each, cols_each)
            rows = pl.multiple_of(col_x * 2 * half_k + half_rows, half_k)
            pltpu.make_async_remote_copy(
                src_ref=weight_h.at[pl.ds(half_rows, half_k), pl.ds(cols, cols_each)],
                dst_ref=weight.at[i, pl.ds(rows, half_k), :],
                send_sem=weight_sem.at[SIDE], recv_sem=weight_sem.at[col_x],
                device_id={"chan": at_x(j)}, device_id_type=MESH,
            ).start()
    for load in halves:
        load.wait()
    for col in range(SPAN):
        rows = pl.ds(col, 2 * SPAN, stride=SPAN)
        block = jnp.concatenate([spectrum[0, rows, :], spectrum[1, rows, :]], axis=1)
        pieces = []
        for part in range(2):
            half = block[part * SPAN:(part + 1) * SPAN]
            pieces += [jnp.where(mask, half, 0.0) for mask in masks]
        spread = jnp.concatenate(pieces, axis=0).astype(BF16)
        wide[pl.ds(col, SEQ, stride=SPAN), :] = dot_t(picked, spread)
    spec_send[...] = wide[...].reshape(SEQ, SPAN, LANES).astype(BF16)
    exchange(spec_send, spec_recv, 1)
    spec_recv[me] = spec_send[me]
    for load in loads[3:]:
        load.wait()
    settled(tok_recv, recv_sem.at[0])
    columns = tok_recv[...].reshape(SEQ * HALF, LANES)
    step = 256

    @pl.loop(0, BLOCK // step)
    def _(i):
        rows = pl.ds(pl.multiple_of(i * step, step), step)
        im_rows = pl.ds(pl.multiple_of(BLOCK + i * step, step), step)
        re, im = dot(forward[rows, :], columns), dot(forward[im_rows, :], columns)
        tr, ti = twist[0, rows, :], twist[1, rows, :]
        pair = jnp.concatenate([re * tr - im * ti, re * ti + im * tr], axis=1).astype(BF16)
        freq[rows, :] = dot(pair, mix[...])

    settled(spec_recv, recv_sem.at[1])

    @pl.loop(0, BLOCK // step)
    def _(i):
        rows = pl.ds(pl.multiple_of(i * step, step), step)
        im_rows = pl.ds(pl.multiple_of(BLOCK + i * step, step), step)
        filt = spec_recv[pl.ds(i * (step // SPAN), step // SPAN)].reshape(step, LANES).astype(F32)
        prod = freq[rows, :LANES] * filt + freq[rows, LANES:] * pltpu.roll(filt, 64, 1)
        back = dot(prod.astype(BF16), unmix[...])
        re, im = back[:, :LANES], back[:, LANES:]
        tr, ti = twist[0, rows, :], twist[1, rows, :]
        turned[rows, :] = (re * tr + im * ti).astype(BF16)
        turned[im_rows, :] = (im * tr - re * ti).astype(BF16)

    for turn in (2, 1, 3, 0):
        first = lax.rem(me // 16 + turn, 4) * 16
        rows = pl.ds(pl.multiple_of(first * HALF, 128), 128)
        conv = dot(inverse[rows, :], turned[...])
        back_send[pl.ds(first, 16)] = conv.reshape(16, HALF, LANES).astype(BF16)

        @pl.loop(0 if turn else 1, 16)
        def _(i):
            peer = first + lax.rem(me + i, 16)
            pltpu.make_async_remote_copy(
                src_ref=back_send.at[peer], dst_ref=back_recv.at[me],
                send_sem=send_sem.at[2], recv_sem=recv_sem.at[2],
                device_id={"seq": peer}, device_id_type=MESH,
            ).start()

    back_recv[me] = back_send[me]

    def weight_half(source, which):
        rows = pl.multiple_of(source * 2 * half_k + which * half_k, half_k)
        return weight.at[:, pl.ds(rows, half_k), :]

    for i in (1, 3, 2):
        source = lax.rem(col_x + i, SIDE)
        mine = weight_half(source, core)
        pltpu.make_async_copy(mine, mine, weight_sem.at[source]).wait()
        pltpu.make_async_remote_copy(
            src_ref=mine, dst_ref=mine, send_sem=pair_sem.at[SIDE], recv_sem=pair_sem.at[source],
            device_id={"seq": sibling}, device_id_type=MESH,
        ).start()

    settled(back_recv, recv_sem.at[2])
    stage[...] = back_recv[...].reshape(SEQ * HALF, LANES).astype(F32)
    chan_row = lax.rem(lax.broadcasted_iota(jnp.int32, (SEQ * OWN, LANES), 0), OWN)
    chan_lane = lax.rem(lax.broadcasted_iota(jnp.int32, (SEQ * OWN, LANES), 1) // SPAN, OWN)
    width = SEQ * OWN
    own_cols = pl.ds(pl.multiple_of(col_x * width, width), width)
    chunk = part_send.shape[3]

    def gated_part(step, source):
        cols = pl.ds(pl.multiple_of(source * width, width), width)
        return gated.at[pl.ds(step * chunk, chunk), cols]

    for low in range(HALF):
        block = stage[pl.ds(low, SEQ, stride=HALF), :].astype(BF16)
        spread = jnp.where(chan_row == chan_lane, dot(pick_t[...], block), 0.0).astype(BF16)
        conv = dot_t(fold[...], spread)
        gate = jnp.concatenate(
            [gate_out[pl.ds((high * HALF + low) * SPAN, SPAN), :] for high in range(2)], axis=0
        ).astype(F32)
        gated[pl.ds(low * 2 * SPAN, 2 * SPAN), own_cols] = (conv * gate).astype(BF16)
        step, done = divmod(low + 1, HALF // 2)
        if done == 0:
            for i in (2, 1, 3):
                pltpu.make_async_remote_copy(
                    src_ref=gated_part(step - 1, col_x), dst_ref=gated_part(step - 1, col_x),
                    send_sem=gated_sem.at[step - 1, SIDE], recv_sem=gated_sem.at[step - 1, col_x],
                    device_id={"chan": at_x(i)}, device_id_type=MESH,
                ).start()
    for i in range(SIDE):
        own_weight(i).wait()
    for i in (1, 3, 2):
        source = lax.rem(col_x + i, SIDE)
        other = weight_half(source, 1 - core)
        pltpu.make_async_copy(other, other, pair_sem.at[source]).wait()

    def pass_on(kind, step, way):
        pltpu.make_async_remote_copy(
            src_ref=part_send.at[kind, step, way], dst_ref=part_recv.at[kind, step, way],
            send_sem=part_sem.at[3, 0, 0], recv_sem=part_sem.at[kind, step, way],
            device_id={"chan": at_y(1 if way == 0 else 3)}, device_id_type=MESH,
        ).start()

    def arrived(kind, step, way):
        ref = part_recv.at[kind, step, way]
        pltpu.make_async_copy(ref, ref, part_sem.at[kind, step, way]).wait()
        return ref[...].astype(F32)

    half_cols = cols_each // 2
    for step in range(2):
        for i in (1, 3, 2):
            part = gated_part(step, lax.rem(col_x + i, SIDE))
            pltpu.make_async_copy(part, part, gated_sem.at[step, lax.rem(col_x + i, SIDE)]).wait()
        rows = pl.ds(step * chunk, chunk)

        def block_half(away, half):
            target = lax.rem(col_y + away, SIDE)
            return dot(gated[rows, :], weight[target, :, pl.ds(half * half_cols, half_cols)])

        for way in range(2):
            part_send[FAR, step, way] = block_half(2, way).astype(BF16)
            pass_on(FAR, step, way)
        for way, away in ((0, 1), (1, 3)):
            part_send[DIRECT, step, way] = block_half(away, 1 - way).astype(BF16)
            pass_on(DIRECT, step, way)
        for way, away in ((0, 1), (1, 3)):
            kept[step, way] = block_half(away, way)
        for half in range(2):
            total[rows, pl.ds(half * half_cols, half_cols)] = block_half(0, half)
    for step in range(2):
        for way in range(2):
            part_send[MERGED, step, way] = (kept[step, way] + arrived(FAR, step, way)).astype(BF16)
            pass_on(MERGED, step, way)
    for step in range(2):
        rows = pl.ds(step * chunk, chunk)
        for way in range(2):
            total[rows, pl.ds((1 - way) * half_cols, half_cols)] += arrived(DIRECT, step, way)
    for step in range(2):
        for way in range(2):
            cols = pl.ds(way * half_cols, half_cols)
            done = total[pl.ds(step * chunk, chunk), cols] + arrived(MERGED, step, way)
            for low in range(HALF // 2):
                for high in range(2):
                    piece = done[(low * 2 + high) * SPAN:(low * 2 + high + 1) * SPAN]
                    place = (high * HALF + step * (HALF // 2) + low) * SPAN
                    out[pl.ds(place, SPAN), cols] = piece.astype(BF16)
    settled(tok_send, send_sem.at[0])
    settled(spec_send, send_sem.at[1])
    settled(back_send, send_sem.at[2])
    three = weight.at[:, pl.ds(0, 3 * half_k), :]
    pltpu.make_async_copy(three, three, weight_sem.at[SIDE]).wait()
    pltpu.make_async_copy(three, three, pair_sem.at[SIDE]).wait()
    for step in range(2):
        sent = gated.at[pl.ds(step * chunk, chunk), pl.ds(0, 3 * width)]
        pltpu.make_async_copy(sent, sent, gated_sem.at[step, SIDE]).wait()
    pltpu.make_async_copy(part_send, part_send, part_sem.at[3, 0, 0]).wait()


def layer(values, gate_in, gate_out, spectrum, out_weight):
    forward, inverse, twist, mix, unmix, pick, pick_t, fold = tables()
    rows, width = values.shape
    cols_each = out_weight.shape[1] // (SIDE * SIDE)
    flat = spectrum.reshape(2 * SPAN * SPAN, width)
    loaded = [(values.shape, BF16)] * 3 + [((2, 2 * SPAN * SPAN, LANES), F32)]
    loaded += [(t.shape, F32 if t.dtype == np.float32 else BF16) for t in
               (forward, inverse, twist, mix, unmix, pick, pick_t, fold)]
    scratch = [pltpu.VMEM(shape, dtype) for shape, dtype in loaded]
    scratch += [
        pltpu.VMEM((SEQ * HALF, LANES), F32),
        pltpu.VMEM((SEQ, HALF, LANES), BF16),
        pltpu.VMEM((SEQ, HALF, LANES), BF16),
        pltpu.VMEM((SEQ * SPAN, LANES), F32),
        pltpu.VMEM((SEQ, SPAN, LANES), BF16),
        pltpu.VMEM((SEQ, SPAN, LANES), BF16),
        pltpu.VMEM((BLOCK, 2 * LANES), F32),
        pltpu.VMEM((2 * BLOCK, LANES), BF16),
        pltpu.VMEM((SEQ, HALF, LANES), BF16),
        pltpu.VMEM((SEQ, HALF, LANES), BF16),
        pltpu.VMEM((SIDE, SIDE * width, cols_each), BF16),
        pltpu.VMEM((rows, SIDE * width), BF16),
        pltpu.VMEM((rows, cols_each), F32),
        pltpu.VMEM((2, 2, rows // 2, cols_each // 2), F32),
        pltpu.VMEM((3, 2, 2, rows // 2, cols_each // 2), BF16),
        pltpu.VMEM((3, 2, 2, rows // 2, cols_each // 2), BF16),
        pltpu.SemaphoreType.DMA((len(loaded) + 1 + SIDE,)),
        pltpu.SemaphoreType.DMA((3,)),
        pltpu.SemaphoreType.DMA((3,)),
        pltpu.SemaphoreType.DMA((SIDE + 1,)),
        pltpu.SemaphoreType.DMA((SIDE + 1,)),
        pltpu.SemaphoreType.DMA((2, SIDE + 1)),
        pltpu.SemaphoreType.DMA((4, 2, 2)),
    ]
    return pl.pallas_call(
        layer_kernel,
        out_shape=jax.ShapeDtypeStruct((rows, cols_each), BF16),
        in_specs=[pl.BlockSpec(memory_space=pltpu.HBM)] * 13,
        out_specs=pl.BlockSpec(memory_space=pltpu.VMEM),
        scratch_shapes=scratch,
        compiler_params=pltpu.CompilerParams(
            collective_id=0, has_side_effects=True, vmem_limit_bytes=60 << 20
        ),
        name="layer",
    )(values, gate_in, gate_out, flat, out_weight, *[jnp.asarray(t) for t in
      (forward, inverse, twist, mix, unmix, pick, pick_t, fold)])


def solution(mesh):
    placed = (
        P("seq", "chan"),
        P("seq", "chan"),
        P("seq", "chan"),
        P(None, None, "seq", "chan"),
        P("chan", None),
    )
    return jax.shard_map(
        layer, mesh=mesh, in_specs=placed, out_specs=P("seq", "chan"), check_vma=False
    )
```

```python
import functools
import math

import jax
import jax.numpy as jnp
import ml_dtypes
import numpy as np
from jax import lax
from jax.experimental import pallas as pl
from jax.experimental.pallas import tpu as pltpu
from jax.sharding import PartitionSpec as P

BLOCK = 1024
SPAN = 16
TOKENS = 16384
SEQ = 64
HALF = 8
LANES = 128
SIDE = 4
OWN = 4
FAR, DIRECT, MERGED = range(3)
STEPS = 4
MESH = pl.DeviceIdType.MESH
BF16 = jnp.bfloat16
F32 = jnp.float32


def tables():
    freq = np.arange(BLOCK)
    base = (16 * np.arange(SEQ)[:, None] + np.arange(HALF)[None, :]).reshape(-1)
    angle = 2.0 * math.pi * ((freq[:, None] * base[None, :]) % BLOCK) / BLOCK
    forward = np.concatenate([np.cos(angle), -np.sin(angle)]).astype(ml_dtypes.bfloat16)
    inverse = np.ascontiguousarray(forward.T)
    lane = np.arange(LANES)
    place = lane % SPAN + 128 * (lane // 64)
    turn = 2.0 * math.pi * ((freq[:, None] * place[None, :]) % TOKENS) / TOKENS
    twist = np.stack([np.cos(turn), -np.sin(turn)]).astype(np.float32)
    span = np.arange(SPAN)
    span_angle = 2.0 * math.pi * ((span[:, None] * span[None, :]) % SPAN) / SPAN
    cos, sin = np.cos(span_angle), np.sin(span_angle)
    same = np.eye(OWN)

    def spread(block):
        return np.kron(same, block)

    re_rows = [np.tile(spread(cos), (2, 1)), np.tile(spread(sin), (2, 1))]
    im_rows = [np.tile(-spread(sin), (2, 1)), np.tile(spread(cos), (2, 1))]
    re, im = np.concatenate(re_rows), np.concatenate(im_rows)
    mix = np.concatenate([re, re, -im, im], axis=1).astype(ml_dtypes.bfloat16)
    back_re = np.concatenate([spread(cos.T), -spread(sin.T)])
    back_im = np.concatenate([spread(sin.T), spread(cos.T)])
    unmix = np.concatenate([back_re, back_re, back_im, back_im], axis=1)
    unmix = (unmix.astype(ml_dtypes.bfloat16).astype(np.float32) / TOKENS).astype(ml_dtypes.bfloat16)
    chan = np.arange(SEQ * OWN)
    pick = (chan[None, :] // OWN == np.arange(SEQ)[:, None]).astype(ml_dtypes.bfloat16)
    pick_t = np.ascontiguousarray(pick.T)
    row = np.arange(2 * SPAN)
    fold = (row[:, None] // SPAN == lane[None, :] // 64) & (row[:, None] % SPAN == lane[None, :] % SPAN)
    fold = fold.astype(ml_dtypes.bfloat16)
    return forward, inverse, twist, mix, unmix, pick, pick_t, fold


def dot(left, right):
    return jnp.dot(left, right, preferred_element_type=F32)


def dot_t(left, right):
    return lax.dot_general(left, right, (((1,), (1,)), ((), ())), preferred_element_type=F32)


def layer_kernel(
    values_h, gate_in_h, gate_out_h, spectrum_h, weight_h, forward_h, inverse_h, twist_h,
    mix_h, unmix_h, pick_h, pick_t_h, fold_h, out,
    values, gate_in, gate_out, spectrum, forward, inverse, twist, mix, unmix, pick, pick_t, fold,
    stage, tok_send, tok_recv, wide, spec_send, spec_recv, freq, turned, back_send, back_recv,
    weight, gated, total, kept, part_send, part_recv,
    load_sem, send_sem, recv_sem, weight_sem, pair_sem, gated_sem, part_sem,
):
    me = lax.axis_index("seq")
    group = lax.axis_index("chan")
    col_x, col_y = lax.rem(group, SIDE), group // SIDE
    core = lax.rem(me, 2)
    sibling = me + 1 - 2 * core
    barrier = pltpu.get_barrier_semaphore()

    def far_first(i):
        return lax.rem(me + SEQ // 2 + ((i + 1) // 2) * (1 - 2 * lax.rem(i, 2)), SEQ)

    @pl.loop(0, SEQ - 1)
    def _(i):
        pl.semaphore_signal(barrier, inc=1, device_id={"seq": far_first(i)}, device_id_type=MESH)

    def at_x(i):
        return col_y * SIDE + lax.rem(col_x + i, SIDE)

    def at_y(i):
        return lax.rem(col_y + i, SIDE) * SIDE + col_x

    for i in range(1, SIDE):
        for peer in (at_x(i), at_y(i)):
            pl.semaphore_signal(barrier, inc=1, device_id={"chan": peer}, device_id_type=MESH)

    sources = (values_h, gate_in_h, pick_h, forward_h, twist_h, mix_h, unmix_h, inverse_h,
               gate_out_h, pick_t_h, fold_h)
    targets = (values, gate_in, pick, forward, twist, mix, unmix, inverse,
               gate_out, pick_t, fold)
    loads = [
        pltpu.make_async_copy(src, dst, load_sem.at[i]) for i, (src, dst) in enumerate(zip(sources, targets))
    ]
    halves = [
        pltpu.make_async_copy(
            spectrum_h.at[:, pl.ds(LANES * i, LANES)], spectrum.at[i], load_sem.at[len(loads) + i]
        )
        for i in range(2)
    ]
    for load in loads[:3] + halves + loads[3:]:
        load.start()
    half_k, cols_each = weight.shape[1] // (2 * SIDE), weight.shape[2]

    def own_weight(i):
        cols = pl.multiple_of((i * SIDE + col_x) * cols_each, cols_each)
        rows = pl.multiple_of(col_x * 2 * half_k, 2 * half_k)
        return pltpu.make_async_copy(
            weight_h.at[:, pl.ds(cols, cols_each)], weight.at[i, pl.ds(rows, 2 * half_k), :],
            load_sem.at[len(loads) + 2 + i],
        )

    for i in range(SIDE):
        own_weight(i).start()
    def exchange(send, recv, slot, quarter):
        @pl.loop(0, SEQ - 1)
        def _(i):
            peer = far_first(i)
            pltpu.make_async_remote_copy(
                src_ref=send.at[peer], dst_ref=recv.at[me],
                send_sem=send_sem.at[slot], recv_sem=recv_sem.at[slot, quarter],
                device_id={"seq": peer}, device_id_type=MESH,
            ).start()

    def settled(ref, sem):
        part = ref.at[pl.ds(0, SEQ - 1)]
        pltpu.make_async_copy(part, part, sem).wait()

    lane = lax.broadcasted_iota(jnp.int32, (SPAN, SEQ * OWN), 1)
    masks = [lax.rem(lane, OWN) == h for h in range(OWN)]
    for load in loads[:3]:
        load.wait()
    picked = pick[...]
    for low in range(HALF):
        pieces = []
        for high in range(2):
            rows = pl.ds((high * HALF + low) * SPAN, SPAN)
            block = (values[rows, :].astype(F32) * gate_in[rows, :].astype(F32)).astype(BF16).astype(F32)
            pieces += [jnp.where(mask, block, 0.0) for mask in masks]
        spread = jnp.concatenate(pieces, axis=0).astype(BF16)
        stage[pl.ds(low, SEQ, stride=HALF), :] = dot_t(picked, spread)
    tok_send[...] = stage[...].reshape(SEQ, HALF, LANES).astype(BF16)
    for load in halves:
        load.wait()
    for col in range(SPAN):
        rows = pl.ds(col, 2 * SPAN, stride=SPAN)
        block = jnp.concatenate([spectrum[0, rows, :], spectrum[1, rows, :]], axis=1)
        pieces = []
        for part in range(2):
            half = block[part * SPAN:(part + 1) * SPAN]
            pieces += [jnp.where(mask, half, 0.0) for mask in masks]
        spread = jnp.concatenate(pieces, axis=0).astype(BF16)
        wide[pl.ds(col, SEQ, stride=SPAN), :] = dot_t(picked, spread)
    spec_send[...] = wide[...].reshape(SEQ, SPAN, LANES).astype(BF16)
    pl.semaphore_wait(barrier, SEQ - 1 + 2 * (SIDE - 1))
    exchange(tok_send, tok_recv, 0, 0)
    tok_recv[me] = tok_send[me]
    exchange(spec_send, spec_recv, 1, me // 16)
    spec_recv[me] = spec_send[me]
    half_rows = pl.multiple_of(core * half_k, half_k)

    @pl.loop(0, SIDE)
    def _(i):
        for j in range(1, SIDE):
            cols = pl.multiple_of((i * SIDE + lax.rem(col_x + j, SIDE)) * cols_each, cols_each)
            rows = pl.multiple_of(col_x * 2 * half_k + half_rows, half_k)
            pltpu.make_async_remote_copy(
                src_ref=weight_h.at[pl.ds(half_rows, half_k), pl.ds(cols, cols_each)],
                dst_ref=weight.at[i, pl.ds(rows, half_k), :],
                send_sem=weight_sem.at[SIDE], recv_sem=weight_sem.at[col_x],
                device_id={"chan": at_x(j)}, device_id_type=MESH,
            ).start()
    for load in loads[3:]:
        load.wait()
    settled(tok_recv, recv_sem.at[0, 0])
    columns = tok_recv[...].reshape(SEQ * HALF, LANES)
    step = 256

    @pl.loop(0, BLOCK // step)
    def _(i):
        rows = pl.ds(pl.multiple_of(i * step, step), step)
        im_rows = pl.ds(pl.multiple_of(BLOCK + i * step, step), step)
        re, im = dot(forward[rows, :], columns), dot(forward[im_rows, :], columns)
        tr, ti = twist[0, rows, :], twist[1, rows, :]
        pair = jnp.concatenate([re * tr - im * ti, re * ti + im * tr], axis=1).astype(BF16)
        freq[rows, :] = dot(pair, mix[...])

    for turn in (2, 1, 3, 0):
        quarter = lax.rem(me // 16 + turn, 4)
        got = spec_recv.at[pl.ds(0, 16 if turn else 15)]
        pltpu.make_async_copy(got, got, recv_sem.at[1, quarter]).wait()
        rows = pl.ds(pl.multiple_of(quarter * step, step), step)
        im_rows = pl.ds(pl.multiple_of(BLOCK + quarter * step, step), step)
        filt = spec_recv[pl.ds(quarter * 16, 16)].reshape(step, LANES).astype(F32)
        prod = freq[rows, :LANES] * filt + freq[rows, LANES:] * pltpu.roll(filt, 64, 1)
        back = dot(prod.astype(BF16), unmix[...])
        re, im = back[:, :LANES], back[:, LANES:]
        tr, ti = twist[0, rows, :], twist[1, rows, :]
        turned[rows, :] = (re * tr + im * ti).astype(BF16)
        turned[im_rows, :] = (im * tr - re * ti).astype(BF16)

    for turn in (2, 1, 3, 0):
        first = lax.rem(me // 16 + turn, 4) * 16
        rows = pl.ds(pl.multiple_of(first * HALF, 128), 128)
        conv = dot(inverse[rows, :], turned[...])
        back_send[pl.ds(first, 16)] = conv.reshape(16, HALF, LANES).astype(BF16)

        @pl.loop(0 if turn else 1, 16)
        def _(i):
            peer = first + lax.rem(me + i, 16)
            pltpu.make_async_remote_copy(
                src_ref=back_send.at[peer], dst_ref=back_recv.at[me],
                send_sem=send_sem.at[2], recv_sem=recv_sem.at[2, 0],
                device_id={"seq": peer}, device_id_type=MESH,
            ).start()

    back_recv[me] = back_send[me]

    def weight_half(source, which):
        rows = pl.multiple_of(source * 2 * half_k + which * half_k, half_k)
        return weight.at[:, pl.ds(rows, half_k), :]

    for i in (1, 3, 2):
        source = lax.rem(col_x + i, SIDE)
        mine = weight_half(source, core)
        pltpu.make_async_copy(mine, mine, weight_sem.at[source]).wait()
        pltpu.make_async_remote_copy(
            src_ref=mine, dst_ref=mine, send_sem=pair_sem.at[SIDE], recv_sem=pair_sem.at[source],
            device_id={"seq": sibling}, device_id_type=MESH,
        ).start()

    settled(back_recv, recv_sem.at[2, 0])
    stage[...] = back_recv[...].reshape(SEQ * HALF, LANES).astype(F32)
    chan_row = lax.rem(lax.broadcasted_iota(jnp.int32, (SEQ * OWN, LANES), 0), OWN)
    chan_lane = lax.rem(lax.broadcasted_iota(jnp.int32, (SEQ * OWN, LANES), 1) // SPAN, OWN)
    width = SEQ * OWN
    own_cols = pl.ds(pl.multiple_of(col_x * width, width), width)
    chunk = part_send.shape[3]

    def gated_part(step, source):
        cols = pl.ds(pl.multiple_of(source * width, width), width)
        return gated.at[pl.ds(step * chunk, chunk), cols]

    for low in range(HALF):
        block = stage[pl.ds(low, SEQ, stride=HALF), :].astype(BF16)
        spread = jnp.where(chan_row == chan_lane, dot(pick_t[...], block), 0.0).astype(BF16)
        conv = dot_t(fold[...], spread)
        gate = jnp.concatenate(
            [gate_out[pl.ds((high * HALF + low) * SPAN, SPAN), :] for high in range(2)], axis=0
        ).astype(F32)
        gated[pl.ds(low * 2 * SPAN, 2 * SPAN), own_cols] = (conv * gate).astype(BF16)
        step, done = divmod(low + 1, HALF // STEPS)
        if done == 0:
            for i in (2, 1, 3):
                pltpu.make_async_remote_copy(
                    src_ref=gated_part(step - 1, col_x), dst_ref=gated_part(step - 1, col_x),
                    send_sem=gated_sem.at[step - 1, SIDE], recv_sem=gated_sem.at[step - 1, col_x],
                    device_id={"chan": at_x(i)}, device_id_type=MESH,
                ).start()
    for i in range(SIDE):
        own_weight(i).wait()
    for i in (1, 3, 2):
        source = lax.rem(col_x + i, SIDE)
        other = weight_half(source, 1 - core)
        pltpu.make_async_copy(other, other, pair_sem.at[source]).wait()

    def pass_on(kind, step, way):
        pltpu.make_async_remote_copy(
            src_ref=part_send.at[kind, step, way], dst_ref=part_recv.at[kind, step, way],
            send_sem=part_sem.at[3, 0, 0], recv_sem=part_sem.at[kind, step, way],
            device_id={"chan": at_y(1 if way == 0 else 3)}, device_id_type=MESH,
        ).start()

    def arrived(kind, step, way):
        ref = part_recv.at[kind, step, way]
        pltpu.make_async_copy(ref, ref, part_sem.at[kind, step, way]).wait()
        return ref[...].astype(F32)

    half_cols = cols_each // 2
    for step in range(STEPS):
        for i in (1, 3, 2):
            part = gated_part(step, lax.rem(col_x + i, SIDE))
            pltpu.make_async_copy(part, part, gated_sem.at[step, lax.rem(col_x + i, SIDE)]).wait()
        rows = pl.ds(step * chunk, chunk)

        def block_half(away, half):
            target = lax.rem(col_y + away, SIDE)
            return dot(gated[rows, :], weight[target, :, pl.ds(half * half_cols, half_cols)])

        for way in range(2):
            part_send[FAR, step, way] = block_half(2, way).astype(BF16)
            pass_on(FAR, step, way)
        for way, away in ((0, 1), (1, 3)):
            part_send[DIRECT, step, way] = block_half(away, 1 - way).astype(BF16)
            pass_on(DIRECT, step, way)
        for way, away in ((0, 1), (1, 3)):
            kept[step, way] = block_half(away, way)
        for half in range(2):
            total[rows, pl.ds(half * half_cols, half_cols)] = block_half(0, half)
    for step in range(STEPS):
        for way in range(2):
            part_send[MERGED, step, way] = (kept[step, way] + arrived(FAR, step, way)).astype(BF16)
            pass_on(MERGED, step, way)
    for step in range(STEPS):
        rows = pl.ds(step * chunk, chunk)
        for way in range(2):
            total[rows, pl.ds((1 - way) * half_cols, half_cols)] += arrived(DIRECT, step, way)
    for step in range(STEPS):
        for way in range(2):
            cols = pl.ds(way * half_cols, half_cols)
            done = total[pl.ds(step * chunk, chunk), cols] + arrived(MERGED, step, way)
            for low in range(HALF // STEPS):
                for high in range(2):
                    piece = done[(low * 2 + high) * SPAN:(low * 2 + high + 1) * SPAN]
                    place = (high * HALF + step * (HALF // STEPS) + low) * SPAN
                    out[pl.ds(place, SPAN), cols] = piece.astype(BF16)
    settled(tok_send, send_sem.at[0])
    settled(spec_send, send_sem.at[1])
    settled(back_send, send_sem.at[2])
    three = weight.at[:, pl.ds(0, 3 * half_k), :]
    pltpu.make_async_copy(three, three, weight_sem.at[SIDE]).wait()
    pltpu.make_async_copy(three, three, pair_sem.at[SIDE]).wait()
    for step in range(STEPS):
        sent = gated.at[pl.ds(step * chunk, chunk), pl.ds(0, 3 * width)]
        pltpu.make_async_copy(sent, sent, gated_sem.at[step, SIDE]).wait()
    pltpu.make_async_copy(part_send, part_send, part_sem.at[3, 0, 0]).wait()


def layer(values, gate_in, gate_out, spectrum, out_weight):
    forward, inverse, twist, mix, unmix, pick, pick_t, fold = tables()
    rows, width = values.shape
    cols_each = out_weight.shape[1] // (SIDE * SIDE)
    flat = spectrum.reshape(2 * SPAN * SPAN, width)
    loaded = [(values.shape, BF16)] * 3 + [((2, 2 * SPAN * SPAN, LANES), F32)]
    loaded += [(t.shape, F32 if t.dtype == np.float32 else BF16) for t in
               (forward, inverse, twist, mix, unmix, pick, pick_t, fold)]
    scratch = [pltpu.VMEM(shape, dtype) for shape, dtype in loaded]
    scratch += [
        pltpu.VMEM((SEQ * HALF, LANES), F32),
        pltpu.VMEM((SEQ, HALF, LANES), BF16),
        pltpu.VMEM((SEQ, HALF, LANES), BF16),
        pltpu.VMEM((SEQ * SPAN, LANES), F32),
        pltpu.VMEM((SEQ, SPAN, LANES), BF16),
        pltpu.VMEM((SEQ, SPAN, LANES), BF16),
        pltpu.VMEM((BLOCK, 2 * LANES), F32),
        pltpu.VMEM((2 * BLOCK, LANES), BF16),
        pltpu.VMEM((SEQ, HALF, LANES), BF16),
        pltpu.VMEM((SEQ, HALF, LANES), BF16),
        pltpu.VMEM((SIDE, SIDE * width, cols_each), BF16),
        pltpu.VMEM((rows, SIDE * width), BF16),
        pltpu.VMEM((rows, cols_each), F32),
        pltpu.VMEM((STEPS, 2, rows // STEPS, cols_each // 2), F32),
        pltpu.VMEM((3, STEPS, 2, rows // STEPS, cols_each // 2), BF16),
        pltpu.VMEM((3, STEPS, 2, rows // STEPS, cols_each // 2), BF16),
        pltpu.SemaphoreType.DMA((len(loaded) + 1 + SIDE,)),
        pltpu.SemaphoreType.DMA((3,)),
        pltpu.SemaphoreType.DMA((3, 4)),
        pltpu.SemaphoreType.DMA((SIDE + 1,)),
        pltpu.SemaphoreType.DMA((SIDE + 1,)),
        pltpu.SemaphoreType.DMA((STEPS, SIDE + 1)),
        pltpu.SemaphoreType.DMA((4, STEPS, 2)),
    ]
    return pl.pallas_call(
        layer_kernel,
        out_shape=jax.ShapeDtypeStruct((rows, cols_each), BF16),
        in_specs=[pl.BlockSpec(memory_space=pltpu.HBM)] * 13,
        out_specs=pl.BlockSpec(memory_space=pltpu.VMEM),
        scratch_shapes=scratch,
        compiler_params=pltpu.CompilerParams(
            collective_id=0, has_side_effects=True, vmem_limit_bytes=60 << 20
        ),
        name="layer",
    )(values, gate_in, gate_out, flat, out_weight, *[jnp.asarray(t) for t in
      (forward, inverse, twist, mix, unmix, pick, pick_t, fold)])


def solution(mesh):
    placed = (
        P("seq", "chan"),
        P("seq", "chan"),
        P("seq", "chan"),
        P(None, None, "seq", "chan"),
        P("chan", None),
    )
    return jax.shard_map(
        layer, mesh=mesh, in_specs=placed, out_specs=P("seq", "chan"), check_vma=False
    )
```

```python
import functools
import math

import jax
import jax.numpy as jnp
import ml_dtypes
import numpy as np
from jax import lax
from jax.experimental import pallas as pl
from jax.experimental.pallas import tpu as pltpu
from jax.sharding import PartitionSpec as P

BLOCK = 1024
SPAN = 16
TOKENS = 16384
SEQ = 64
HALF = 8
LANES = 128
SIDE = 4
OWN = 4
FAR, DIRECT, MERGED = range(3)
STEPS = 4
MESH = pl.DeviceIdType.MESH
BF16 = jnp.bfloat16
F32 = jnp.float32


def tables():
    freq = np.arange(BLOCK)
    base = (16 * np.arange(SEQ)[:, None] + np.arange(HALF)[None, :]).reshape(-1)
    angle = 2.0 * math.pi * ((freq[:, None] * base[None, :]) % BLOCK) / BLOCK
    forward = np.concatenate([np.cos(angle), -np.sin(angle)]).astype(ml_dtypes.bfloat16)
    inverse = np.ascontiguousarray(forward.T)
    lane = np.arange(LANES)
    place = lane % SPAN + 128 * (lane // 64)
    turn = 2.0 * math.pi * ((freq[:, None] * place[None, :]) % TOKENS) / TOKENS
    twist = np.stack([np.cos(turn), -np.sin(turn)]).astype(np.float32)
    span = np.arange(SPAN)
    span_angle = 2.0 * math.pi * ((span[:, None] * span[None, :]) % SPAN) / SPAN
    cos, sin = np.cos(span_angle), np.sin(span_angle)
    same = np.eye(OWN)

    def spread(block):
        return np.kron(same, block)

    re_rows = [np.tile(spread(cos), (2, 1)), np.tile(spread(sin), (2, 1))]
    im_rows = [np.tile(-spread(sin), (2, 1)), np.tile(spread(cos), (2, 1))]
    re, im = np.concatenate(re_rows), np.concatenate(im_rows)
    mix = np.concatenate([re, re, -im, im], axis=1).astype(ml_dtypes.bfloat16)
    back_re = np.concatenate([spread(cos.T), -spread(sin.T)])
    back_im = np.concatenate([spread(sin.T), spread(cos.T)])
    unmix = np.concatenate([back_re, back_re, back_im, back_im], axis=1)
    unmix = (unmix.astype(ml_dtypes.bfloat16).astype(np.float32) / TOKENS).astype(ml_dtypes.bfloat16)
    chan = np.arange(SEQ * OWN)
    pick = (chan[None, :] // OWN == np.arange(SEQ)[:, None]).astype(ml_dtypes.bfloat16)
    pick_t = np.ascontiguousarray(pick.T)
    row = np.arange(2 * SPAN)
    fold = (row[:, None] // SPAN == lane[None, :] // 64) & (row[:, None] % SPAN == lane[None, :] % SPAN)
    fold = fold.astype(ml_dtypes.bfloat16)
    return forward, inverse, twist, mix, unmix, pick, pick_t, fold


def dot(left, right):
    return jnp.dot(left, right, preferred_element_type=F32)


def dot_t(left, right):
    return lax.dot_general(left, right, (((1,), (1,)), ((), ())), preferred_element_type=F32)


def layer_kernel(
    values_h, gate_in_h, gate_out_h, spectrum_h, weight_h, forward_h, inverse_h, twist_h,
    mix_h, unmix_h, pick_h, pick_t_h, fold_h, out,
    values, gate_in, gate_out, spectrum, forward, inverse, twist, mix, unmix, pick, pick_t, fold,
    stage, tok_send, tok_recv, wide, spec_send, spec_recv, freq, turned, back_send, back_recv,
    weight, gated, total, kept, part_send, part_recv,
    load_sem, send_sem, recv_sem, weight_sem, pair_sem, gated_sem, part_sem,
):
    me = lax.axis_index("seq")
    group = lax.axis_index("chan")
    col_x, col_y = lax.rem(group, SIDE), group // SIDE
    core = lax.rem(me, 2)
    sibling = me + 1 - 2 * core
    barrier = pltpu.get_barrier_semaphore()

    def far_first(i):
        return lax.rem(me + SEQ // 2 + ((i + 1) // 2) * (1 - 2 * lax.rem(i, 2)), SEQ)

    @pl.loop(0, SEQ - 1)
    def _(i):
        pl.semaphore_signal(barrier, inc=1, device_id={"seq": far_first(i)}, device_id_type=MESH)

    def at_x(i):
        return col_y * SIDE + lax.rem(col_x + i, SIDE)

    def at_y(i):
        return lax.rem(col_y + i, SIDE) * SIDE + col_x

    for i in range(1, SIDE):
        for peer in (at_x(i), at_y(i)):
            pl.semaphore_signal(barrier, inc=1, device_id={"chan": peer}, device_id_type=MESH)

    sources = (values_h, gate_in_h, pick_h, forward_h, twist_h, mix_h, unmix_h, inverse_h,
               gate_out_h, pick_t_h, fold_h)
    targets = (values, gate_in, pick, forward, twist, mix, unmix, inverse,
               gate_out, pick_t, fold)
    loads = [
        pltpu.make_async_copy(src, dst, load_sem.at[i]) for i, (src, dst) in enumerate(zip(sources, targets))
    ]
    halves = [
        pltpu.make_async_copy(
            spectrum_h.at[:, pl.ds(LANES * i, LANES)], spectrum.at[i], load_sem.at[len(loads) + i]
        )
        for i in range(2)
    ]
    for load in loads[:3] + halves + loads[3:]:
        load.start()
    half_k, cols_each = weight.shape[1] // (2 * SIDE), weight.shape[2]

    def own_weight(i):
        cols = pl.multiple_of((i * SIDE + col_x) * cols_each, cols_each)
        rows = pl.multiple_of(col_x * 2 * half_k, 2 * half_k)
        return pltpu.make_async_copy(
            weight_h.at[:, pl.ds(cols, cols_each)], weight.at[i, pl.ds(rows, 2 * half_k), :],
            load_sem.at[len(loads) + 2 + i],
        )

    for i in range(SIDE):
        own_weight(i).start()
    def exchange(send, recv, slot, quarter):
        @pl.loop(0, SEQ - 1)
        def _(i):
            peer = far_first(i)
            pltpu.make_async_remote_copy(
                src_ref=send.at[peer], dst_ref=recv.at[me],
                send_sem=send_sem.at[slot], recv_sem=recv_sem.at[slot, quarter],
                device_id={"seq": peer}, device_id_type=MESH,
            ).start()

    def settled(ref, sem):
        part = ref.at[pl.ds(0, SEQ - 1)]
        pltpu.make_async_copy(part, part, sem).wait()

    lane = lax.broadcasted_iota(jnp.int32, (SPAN, SEQ * OWN), 1)
    masks = [lax.rem(lane, OWN) == h for h in range(OWN)]
    for load in loads[:3]:
        load.wait()
    picked = pick[...]
    for low in range(HALF):
        pieces = []
        for high in range(2):
            rows = pl.ds((high * HALF + low) * SPAN, SPAN)
            block = (values[rows, :].astype(F32) * gate_in[rows, :].astype(F32)).astype(BF16).astype(F32)
            pieces += [jnp.where(mask, block, 0.0) for mask in masks]
        spread = jnp.concatenate(pieces, axis=0).astype(BF16)
        stage[pl.ds(low, SEQ, stride=HALF), :] = dot_t(picked, spread)
    tok_send[...] = stage[...].reshape(SEQ, HALF, LANES).astype(BF16)
    for load in halves:
        load.wait()
    for col in range(SPAN):
        rows = pl.ds(col, 2 * SPAN, stride=SPAN)
        block = jnp.concatenate([spectrum[0, rows, :], spectrum[1, rows, :]], axis=1)
        pieces = []
        for part in range(2):
            half = block[part * SPAN:(part + 1) * SPAN]
            pieces += [jnp.where(mask, half, 0.0) for mask in masks]
        spread = jnp.concatenate(pieces, axis=0).astype(BF16)
        wide[pl.ds(col, SEQ, stride=SPAN), :] = dot_t(picked, spread)
    spec_send[...] = wide[...].reshape(SEQ, SPAN, LANES).astype(BF16)
    pl.semaphore_wait(barrier, SEQ - 1 + 2 * (SIDE - 1))
    exchange(tok_send, tok_recv, 0, 0)
    tok_recv[me] = tok_send[me]
    exchange(spec_send, spec_recv, 1, me // 16)
    spec_recv[me] = spec_send[me]
    half_rows = pl.multiple_of(core * half_k, half_k)

    @pl.loop(0, SIDE)
    def _(i):
        for j in range(1, SIDE):
            cols = pl.multiple_of((i * SIDE + lax.rem(col_x + j, SIDE)) * cols_each, cols_each)
            rows = pl.multiple_of(col_x * 2 * half_k + half_rows, half_k)
            pltpu.make_async_remote_copy(
                src_ref=weight_h.at[pl.ds(half_rows, half_k), pl.ds(cols, cols_each)],
                dst_ref=weight.at[i, pl.ds(rows, half_k), :],
                send_sem=weight_sem.at[SIDE], recv_sem=weight_sem.at[col_x],
                device_id={"chan": at_x(j)}, device_id_type=MESH,
            ).start()
    for load in loads[3:]:
        load.wait()
    settled(tok_recv, recv_sem.at[0, 0])
    columns = tok_recv[...].reshape(SEQ * HALF, LANES)
    step = 256

    @pl.loop(0, BLOCK // step)
    def _(i):
        rows = pl.ds(pl.multiple_of(i * step, step), step)
        im_rows = pl.ds(pl.multiple_of(BLOCK + i * step, step), step)
        re, im = dot(forward[rows, :], columns), dot(forward[im_rows, :], columns)
        tr, ti = twist[0, rows, :], twist[1, rows, :]
        pair = jnp.concatenate([re * tr - im * ti, re * ti + im * tr], axis=1).astype(BF16)
        freq[rows, :] = dot(pair, mix[...])

    for turn in (2, 1, 3, 0):
        quarter = lax.rem(me // 16 + turn, 4)
        got = spec_recv.at[pl.ds(0, 16 if turn else 15)]
        pltpu.make_async_copy(got, got, recv_sem.at[1, quarter]).wait()
        rows = pl.ds(pl.multiple_of(quarter * step, step), step)
        im_rows = pl.ds(pl.multiple_of(BLOCK + quarter * step, step), step)
        filt = spec_recv[pl.ds(quarter * 16, 16)].reshape(step, LANES).astype(F32)
        prod = freq[rows, :LANES] * filt + freq[rows, LANES:] * pltpu.roll(filt, 64, 1)
        back = dot(prod.astype(BF16), unmix[...])
        re, im = back[:, :LANES], back[:, LANES:]
        tr, ti = twist[0, rows, :], twist[1, rows, :]
        turned[rows, :] = (re * tr + im * ti).astype(BF16)
        turned[im_rows, :] = (im * tr - re * ti).astype(BF16)

    for turn in (2, 1, 3, 0):
        first = lax.rem(me // 16 + turn, 4) * 16
        rows = pl.ds(pl.multiple_of(first * HALF, 128), 128)
        conv = dot(inverse[rows, :], turned[...])
        back_send[pl.ds(first, 16)] = conv.reshape(16, HALF, LANES).astype(BF16)

        @pl.loop(0 if turn else 1, 16)
        def _(i):
            peer = first + lax.rem(me + i, 16)
            pltpu.make_async_remote_copy(
                src_ref=back_send.at[peer], dst_ref=back_recv.at[me],
                send_sem=send_sem.at[2], recv_sem=recv_sem.at[2, 0],
                device_id={"seq": peer}, device_id_type=MESH,
            ).start()

    back_recv[me] = back_send[me]

    def weight_half(source, which):
        rows = pl.multiple_of(source * 2 * half_k + which * half_k, half_k)
        return weight.at[:, pl.ds(rows, half_k), :]

    for i in (1, 3, 2):
        source = lax.rem(col_x + i, SIDE)
        mine = weight_half(source, core)
        pltpu.make_async_copy(mine, mine, weight_sem.at[source]).wait()
        pltpu.make_async_remote_copy(
            src_ref=mine, dst_ref=mine, send_sem=pair_sem.at[SIDE], recv_sem=pair_sem.at[source],
            device_id={"seq": sibling}, device_id_type=MESH,
        ).start()

    settled(back_recv, recv_sem.at[2, 0])
    stage[...] = back_recv[...].reshape(SEQ * HALF, LANES).astype(F32)
    chan_row = lax.rem(lax.broadcasted_iota(jnp.int32, (SEQ * OWN, LANES), 0), OWN)
    chan_lane = lax.rem(lax.broadcasted_iota(jnp.int32, (SEQ * OWN, LANES), 1) // SPAN, OWN)
    width = SEQ * OWN
    own_cols = pl.ds(pl.multiple_of(col_x * width, width), width)
    chunk = part_send.shape[3]

    def gated_part(step, source):
        cols = pl.ds(pl.multiple_of(source * width, width), width)
        return gated.at[pl.ds(step * chunk, chunk), cols]

    for low in range(HALF):
        block = stage[pl.ds(low, SEQ, stride=HALF), :].astype(BF16)
        spread = jnp.where(chan_row == chan_lane, dot(pick_t[...], block), 0.0).astype(BF16)
        conv = dot_t(fold[...], spread)
        gate = jnp.concatenate(
            [gate_out[pl.ds((high * HALF + low) * SPAN, SPAN), :] for high in range(2)], axis=0
        ).astype(F32)
        gated[pl.ds(low * 2 * SPAN, 2 * SPAN), own_cols] = (conv * gate).astype(BF16)
        step, done = divmod(low + 1, HALF // STEPS)
        if done == 0:
            for i in (2, 1, 3):
                pltpu.make_async_remote_copy(
                    src_ref=gated_part(step - 1, col_x), dst_ref=gated_part(step - 1, col_x),
                    send_sem=gated_sem.at[step - 1, SIDE], recv_sem=gated_sem.at[step - 1, col_x],
                    device_id={"chan": at_x(i)}, device_id_type=MESH,
                ).start()
    for i in range(SIDE):
        own_weight(i).wait()
    for i in (1, 3, 2):
        source = lax.rem(col_x + i, SIDE)
        other = weight_half(source, 1 - core)
        pltpu.make_async_copy(other, other, pair_sem.at[source]).wait()

    def pass_on(kind, step, way):
        pltpu.make_async_remote_copy(
            src_ref=part_send.at[kind, step, way], dst_ref=part_recv.at[kind, step, way],
            send_sem=part_sem.at[3, 0, 0], recv_sem=part_sem.at[kind, step, way],
            device_id={"chan": at_y(1 if way == 0 else 3)}, device_id_type=MESH,
        ).start()

    def arrived(kind, step, way):
        ref = part_recv.at[kind, step, way]
        pltpu.make_async_copy(ref, ref, part_sem.at[kind, step, way]).wait()
        return ref[...].astype(F32)

    half_cols = cols_each // 2
    for step in range(STEPS):
        for i in (1, 3, 2):
            part = gated_part(step, lax.rem(col_x + i, SIDE))
            pltpu.make_async_copy(part, part, gated_sem.at[step, lax.rem(col_x + i, SIDE)]).wait()
        rows = pl.ds(step * chunk, chunk)

        def block_half(away, half):
            target = lax.rem(col_y + away, SIDE)
            return dot(gated[rows, :], weight[target, :, pl.ds(half * half_cols, half_cols)])

        for way in range(2):
            part_send[FAR, step, way] = block_half(2, way).astype(BF16)
            pass_on(FAR, step, way)
        for way, away in ((0, 1), (1, 3)):
            part_send[DIRECT, step, way] = block_half(away, 1 - way).astype(BF16)
            pass_on(DIRECT, step, way)
        for way, away in ((0, 1), (1, 3)):
            kept[step, way] = block_half(away, way)
        for half in range(2):
            total[rows, pl.ds(half * half_cols, half_cols)] = block_half(0, half)
    for step in range(STEPS):
        for way in range(2):
            part_send[MERGED, step, way] = (kept[step, way] + arrived(FAR, step, way)).astype(BF16)
            pass_on(MERGED, step, way)
    for step in range(STEPS):
        rows = pl.ds(step * chunk, chunk)
        for way in range(2):
            total[rows, pl.ds((1 - way) * half_cols, half_cols)] += arrived(DIRECT, step, way)
    for step in range(STEPS):
        for way in range(2):
            cols = pl.ds(way * half_cols, half_cols)
            done = total[pl.ds(step * chunk, chunk), cols] + arrived(MERGED, step, way)
            for low in range(HALF // STEPS):
                for high in range(2):
                    piece = done[(low * 2 + high) * SPAN:(low * 2 + high + 1) * SPAN]
                    place = (high * HALF + step * (HALF // STEPS) + low) * SPAN
                    out[pl.ds(place, SPAN), cols] = piece.astype(BF16)
    settled(tok_send, send_sem.at[0])
    settled(spec_send, send_sem.at[1])
    settled(back_send, send_sem.at[2])
    three = weight.at[:, pl.ds(0, 3 * half_k), :]
    pltpu.make_async_copy(three, three, weight_sem.at[SIDE]).wait()
    pltpu.make_async_copy(three, three, pair_sem.at[SIDE]).wait()
    for step in range(STEPS):
        sent = gated.at[pl.ds(step * chunk, chunk), pl.ds(0, 3 * width)]
        pltpu.make_async_copy(sent, sent, gated_sem.at[step, SIDE]).wait()
    pltpu.make_async_copy(part_send, part_send, part_sem.at[3, 0, 0]).wait()


def layer(values, gate_in, gate_out, spectrum, out_weight):
    forward, inverse, twist, mix, unmix, pick, pick_t, fold = tables()
    rows, width = values.shape
    cols_each = out_weight.shape[1] // (SIDE * SIDE)
    flat = spectrum.reshape(2 * SPAN * SPAN, width)
    loaded = [(values.shape, BF16)] * 3 + [((2, 2 * SPAN * SPAN, LANES), F32)]
    loaded += [(t.shape, F32 if t.dtype == np.float32 else BF16) for t in
               (forward, inverse, twist, mix, unmix, pick, pick_t, fold)]
    scratch = [pltpu.VMEM(shape, dtype) for shape, dtype in loaded]
    scratch += [
        pltpu.VMEM((SEQ * HALF, LANES), F32),
        pltpu.VMEM((SEQ, HALF, LANES), BF16),
        pltpu.VMEM((SEQ, HALF, LANES), BF16),
        pltpu.VMEM((SEQ * SPAN, LANES), F32),
        pltpu.VMEM((SEQ, SPAN, LANES), BF16),
        pltpu.VMEM((SEQ, SPAN, LANES), BF16),
        pltpu.VMEM((BLOCK, 2 * LANES), F32),
        pltpu.VMEM((2 * BLOCK, LANES), BF16),
        pltpu.VMEM((SEQ, HALF, LANES), BF16),
        pltpu.VMEM((SEQ, HALF, LANES), BF16),
        pltpu.VMEM((SIDE, SIDE * width, cols_each), BF16),
        pltpu.VMEM((rows, SIDE * width), BF16),
        pltpu.VMEM((rows, cols_each), F32),
        pltpu.VMEM((STEPS, 2, rows // STEPS, cols_each // 2), F32),
        pltpu.VMEM((3, STEPS, 2, rows // STEPS, cols_each // 2), BF16),
        pltpu.VMEM((3, STEPS, 2, rows // STEPS, cols_each // 2), BF16),
        pltpu.SemaphoreType.DMA((len(loaded) + 1 + SIDE,)),
        pltpu.SemaphoreType.DMA((3,)),
        pltpu.SemaphoreType.DMA((3, 4)),
        pltpu.SemaphoreType.DMA((SIDE + 1,)),
        pltpu.SemaphoreType.DMA((SIDE + 1,)),
        pltpu.SemaphoreType.DMA((STEPS, SIDE + 1)),
        pltpu.SemaphoreType.DMA((4, STEPS, 2)),
    ]
    return pl.pallas_call(
        layer_kernel,
        out_shape=jax.ShapeDtypeStruct((rows, cols_each), BF16),
        in_specs=[pl.BlockSpec(memory_space=pltpu.HBM)] * 13,
        out_specs=pl.BlockSpec(memory_space=pltpu.VMEM),
        scratch_shapes=scratch,
        compiler_params=pltpu.CompilerParams(
            collective_id=0, has_side_effects=True, vmem_limit_bytes=32 << 20
        ),
        name="layer",
    )(*[
        pltpu.with_memory_space_constraint(t, pltpu.HBM)
        for t in (values, gate_in, gate_out, flat, out_weight)
    ], *[
        pltpu.with_memory_space_constraint(jnp.asarray(t), pltpu.HBM)
        for t in (forward, inverse, twist, mix, unmix, pick, pick_t, fold)
    ])


def solution(mesh):
    placed = (
        P("seq", "chan"),
        P("seq", "chan"),
        P("seq", "chan"),
        P(None, None, "seq", "chan"),
        P("chan", None),
    )
    return jax.shard_map(
        layer, mesh=mesh, in_specs=placed, out_specs=P("seq", "chan"), check_vma=False
    )
```

```python
import functools
import math

import jax
import jax.numpy as jnp
import ml_dtypes
import numpy as np
from jax import lax
from jax.experimental import pallas as pl
from jax.experimental.pallas import tpu as pltpu
from jax.sharding import PartitionSpec as P

BLOCK = 1024
SPAN = 16
TOKENS = 16384
SEQ = 64
HALF = 8
LANES = 128
SIDE = 4
OWN = 4
FAR, DIRECT, MERGED = range(3)
STEPS = 4
MESH = pl.DeviceIdType.MESH
BF16 = jnp.bfloat16
F32 = jnp.float32


def tables():
    freq = np.arange(BLOCK)
    base = (16 * np.arange(SEQ)[:, None] + np.arange(HALF)[None, :]).reshape(-1)
    angle = 2.0 * math.pi * ((freq[:, None] * base[None, :]) % BLOCK) / BLOCK
    forward = np.concatenate([np.cos(angle), -np.sin(angle)]).astype(ml_dtypes.bfloat16)
    inverse = np.ascontiguousarray(forward.T)
    lane = np.arange(LANES)
    place = lane % SPAN + 128 * (lane // 64)
    turn = 2.0 * math.pi * ((freq[:, None] * place[None, :]) % TOKENS) / TOKENS
    twist = np.stack([np.cos(turn), -np.sin(turn)]).astype(np.float32)
    span = np.arange(SPAN)
    span_angle = 2.0 * math.pi * ((span[:, None] * span[None, :]) % SPAN) / SPAN
    cos, sin = np.cos(span_angle), np.sin(span_angle)
    same = np.eye(OWN)

    def spread(block):
        return np.kron(same, block)

    re_rows = [np.tile(spread(cos), (2, 1)), np.tile(spread(sin), (2, 1))]
    im_rows = [np.tile(-spread(sin), (2, 1)), np.tile(spread(cos), (2, 1))]
    re, im = np.concatenate(re_rows), np.concatenate(im_rows)
    mix = np.concatenate([re, re, -im, im], axis=1).astype(ml_dtypes.bfloat16)
    back_re = np.concatenate([spread(cos.T), -spread(sin.T)])
    back_im = np.concatenate([spread(sin.T), spread(cos.T)])
    unmix = np.concatenate([back_re, back_re, back_im, back_im], axis=1)
    unmix = (unmix.astype(ml_dtypes.bfloat16).astype(np.float32) / TOKENS).astype(ml_dtypes.bfloat16)
    chan = np.arange(SEQ * OWN)
    pick = (chan[None, :] // OWN == np.arange(SEQ)[:, None]).astype(ml_dtypes.bfloat16)
    pick_t = np.ascontiguousarray(pick.T)
    row = np.arange(2 * SPAN)
    fold = (row[:, None] // SPAN == lane[None, :] // 64) & (row[:, None] % SPAN == lane[None, :] % SPAN)
    fold = fold.astype(ml_dtypes.bfloat16)
    return forward, inverse, twist, mix, unmix, pick, pick_t, fold


def dot(left, right):
    return jnp.dot(left, right, preferred_element_type=F32)


def dot_t(left, right):
    return lax.dot_general(left, right, (((1,), (1,)), ((), ())), preferred_element_type=F32)


def layer_kernel(
    values_h, gate_in_h, gate_out_h, spectrum_h, weight_h, forward_h, inverse_h, twist_h,
    mix_h, unmix_h, pick_h, pick_t_h, fold_h, out,
    values, gate_in, gate_out, spectrum, forward, inverse, twist, mix, unmix, pick, pick_t, fold,
    stage, tok_send, tok_recv, wide, spec_send, spec_recv, freq, turned, back_send, back_recv,
    weight, gated, total, kept, part_send, part_recv,
    load_sem, send_sem, recv_sem, weight_sem, pair_sem, gated_sem, part_sem,
):
    me = lax.axis_index("seq")
    group = lax.axis_index("chan")
    col_x, col_y = lax.rem(group, SIDE), group // SIDE
    core = lax.rem(me, 2)
    sibling = me + 1 - 2 * core
    barrier = pltpu.get_barrier_semaphore()

    def far_first(i):
        return lax.rem(me + SEQ // 2 + ((i + 1) // 2) * (1 - 2 * lax.rem(i, 2)), SEQ)

    @pl.loop(0, SEQ - 1)
    def _(i):
        pl.semaphore_signal(barrier, inc=1, device_id={"seq": far_first(i)}, device_id_type=MESH)

    def at_x(i):
        return col_y * SIDE + lax.rem(col_x + i, SIDE)

    def at_y(i):
        return lax.rem(col_y + i, SIDE) * SIDE + col_x

    for i in range(1, SIDE):
        for peer in (at_x(i), at_y(i)):
            pl.semaphore_signal(barrier, inc=1, device_id={"chan": peer}, device_id_type=MESH)

    sources = (values_h, gate_in_h, pick_h, forward_h, twist_h, mix_h, unmix_h, inverse_h,
               gate_out_h, pick_t_h, fold_h)
    targets = (values, gate_in, pick, forward, twist, mix, unmix, inverse,
               gate_out, pick_t, fold)
    loads = [
        pltpu.make_async_copy(src, dst, load_sem.at[i]) for i, (src, dst) in enumerate(zip(sources, targets))
    ]
    halves = [
        pltpu.make_async_copy(
            spectrum_h.at[:, pl.ds(LANES * i, LANES)], spectrum.at[i], load_sem.at[len(loads) + i]
        )
        for i in range(2)
    ]
    for load in loads[:3] + halves + loads[3:]:
        load.start()
    half_k, cols_each = weight.shape[1] // (2 * SIDE), weight.shape[2]

    def own_weight(i):
        cols = pl.multiple_of((i * SIDE + col_x) * cols_each, cols_each)
        rows = pl.multiple_of(col_x * 2 * half_k, 2 * half_k)
        return pltpu.make_async_copy(
            weight_h.at[:, pl.ds(cols, cols_each)], weight.at[i, pl.ds(rows, 2 * half_k), :],
            load_sem.at[len(loads) + 2 + i],
        )

    for i in range(SIDE):
        own_weight(i).start()
    def exchange(send, recv, slot, quarter):
        @pl.loop(0, SEQ - 1)
        def _(i):
            peer = far_first(i)
            pltpu.make_async_remote_copy(
                src_ref=send.at[peer], dst_ref=recv.at[me],
                send_sem=send_sem.at[slot], recv_sem=recv_sem.at[slot, quarter],
                device_id={"seq": peer}, device_id_type=MESH,
            ).start()

    def settled(ref, sem):
        part = ref.at[pl.ds(0, SEQ - 1)]
        pltpu.make_async_copy(part, part, sem).wait()

    lane = lax.broadcasted_iota(jnp.int32, (SPAN, SEQ * OWN), 1)
    masks = [lax.rem(lane, OWN) == h for h in range(OWN)]
    for load in loads[:3]:
        load.wait()
    picked = pick[...]
    for low in range(HALF):
        pieces = []
        for high in range(2):
            rows = pl.ds((high * HALF + low) * SPAN, SPAN)
            block = (values[rows, :].astype(F32) * gate_in[rows, :].astype(F32)).astype(BF16).astype(F32)
            pieces += [jnp.where(mask, block, 0.0) for mask in masks]
        spread = jnp.concatenate(pieces, axis=0).astype(BF16)
        stage[pl.ds(low, SEQ, stride=HALF), :] = dot_t(picked, spread)
    tok_send[...] = stage[...].reshape(SEQ, HALF, LANES).astype(BF16)
    for load in halves:
        load.wait()
    for col in range(SPAN):
        rows = pl.ds(col, 2 * SPAN, stride=SPAN)
        block = jnp.concatenate([spectrum[0, rows, :], spectrum[1, rows, :]], axis=1)
        pieces = []
        for part in range(2):
            half = block[part * SPAN:(part + 1) * SPAN]
            pieces += [jnp.where(mask, half, 0.0) for mask in masks]
        spread = jnp.concatenate(pieces, axis=0).astype(BF16)
        wide[pl.ds(col, SEQ, stride=SPAN), :] = dot_t(picked, spread)
    spec_send[...] = wide[...].reshape(SEQ, SPAN, LANES).astype(BF16)
    pl.semaphore_wait(barrier, SEQ - 1 + 2 * (SIDE - 1))
    exchange(tok_send, tok_recv, 0, 0)
    tok_recv[me] = tok_send[me]
    exchange(spec_send, spec_recv, 1, me // 16)
    spec_recv[me] = spec_send[me]
    half_rows = pl.multiple_of(core * half_k, half_k)

    @pl.loop(0, SIDE)
    def _(i):
        for j in range(1, SIDE):
            cols = pl.multiple_of((i * SIDE + lax.rem(col_x + j, SIDE)) * cols_each, cols_each)
            rows = pl.multiple_of(col_x * 2 * half_k + half_rows, half_k)
            pltpu.make_async_remote_copy(
                src_ref=weight_h.at[pl.ds(half_rows, half_k), pl.ds(cols, cols_each)],
                dst_ref=weight.at[i, pl.ds(rows, half_k), :],
                send_sem=weight_sem.at[SIDE], recv_sem=weight_sem.at[col_x],
                device_id={"chan": at_x(j)}, device_id_type=MESH,
            ).start()
    for load in loads[3:]:
        load.wait()
    settled(tok_recv, recv_sem.at[0, 0])
    columns = tok_recv[...].reshape(SEQ * HALF, LANES)
    step = 256

    @pl.loop(0, BLOCK // step)
    def _(i):
        rows = pl.ds(pl.multiple_of(i * step, step), step)
        im_rows = pl.ds(pl.multiple_of(BLOCK + i * step, step), step)
        re, im = dot(forward[rows, :], columns), dot(forward[im_rows, :], columns)
        tr, ti = twist[0, rows, :], twist[1, rows, :]
        pair = jnp.concatenate([re * tr - im * ti, re * ti + im * tr], axis=1).astype(BF16)
        freq[rows, :] = dot(pair, mix[...])

    for turn in (2, 1, 3, 0):
        quarter = lax.rem(me // 16 + turn, 4)
        got = spec_recv.at[pl.ds(0, 16 if turn else 15)]
        pltpu.make_async_copy(got, got, recv_sem.at[1, quarter]).wait()
        rows = pl.ds(pl.multiple_of(quarter * step, step), step)
        im_rows = pl.ds(pl.multiple_of(BLOCK + quarter * step, step), step)
        filt = spec_recv[pl.ds(quarter * 16, 16)].reshape(step, LANES).astype(F32)
        prod = freq[rows, :LANES] * filt + freq[rows, LANES:] * pltpu.roll(filt, 64, 1)
        back = dot(prod.astype(BF16), unmix[...])
        re, im = back[:, :LANES], back[:, LANES:]
        tr, ti = twist[0, rows, :], twist[1, rows, :]
        turned[rows, :] = (re * tr + im * ti).astype(BF16)
        turned[im_rows, :] = (im * tr - re * ti).astype(BF16)

    for turn in (2, 1, 3, 0):
        first = lax.rem(me // 16 + turn, 4) * 16
        rows = pl.ds(pl.multiple_of(first * HALF, 128), 128)
        conv = dot(inverse[rows, :], turned[...])
        back_send[pl.ds(first, 16)] = conv.reshape(16, HALF, LANES).astype(BF16)

        @pl.loop(0 if turn else 1, 16)
        def _(i):
            peer = first + lax.rem(me + i, 16)
            pltpu.make_async_remote_copy(
                src_ref=back_send.at[peer], dst_ref=back_recv.at[me],
                send_sem=send_sem.at[2], recv_sem=recv_sem.at[2, 0],
                device_id={"seq": peer}, device_id_type=MESH,
            ).start()

    back_recv[me] = back_send[me]

    def weight_half(source, which):
        rows = pl.multiple_of(source * 2 * half_k + which * half_k, half_k)
        return weight.at[:, pl.ds(rows, half_k), :]

    settled(back_recv, recv_sem.at[2, 0])
    stage[...] = back_recv[...].reshape(SEQ * HALF, LANES).astype(F32)
    chan_row = lax.rem(lax.broadcasted_iota(jnp.int32, (SEQ * OWN, LANES), 0), OWN)
    chan_lane = lax.rem(lax.broadcasted_iota(jnp.int32, (SEQ * OWN, LANES), 1) // SPAN, OWN)
    width = SEQ * OWN
    own_cols = pl.ds(pl.multiple_of(col_x * width, width), width)
    chunk = part_send.shape[3]

    def gated_part(step, source):
        cols = pl.ds(pl.multiple_of(source * width, width), width)
        return gated.at[pl.ds(step * chunk, chunk), cols]

    for low in range(HALF):
        block = stage[pl.ds(low, SEQ, stride=HALF), :].astype(BF16)
        spread = jnp.where(chan_row == chan_lane, dot(pick_t[...], block), 0.0).astype(BF16)
        conv = dot_t(fold[...], spread)
        gate = jnp.concatenate(
            [gate_out[pl.ds((high * HALF + low) * SPAN, SPAN), :] for high in range(2)], axis=0
        ).astype(F32)
        gated[pl.ds(low * 2 * SPAN, 2 * SPAN), own_cols] = (conv * gate).astype(BF16)
        step, done = divmod(low + 1, HALF // STEPS)
        if done == 0:
            for i in (2, 1, 3):
                pltpu.make_async_remote_copy(
                    src_ref=gated_part(step - 1, col_x), dst_ref=gated_part(step - 1, col_x),
                    send_sem=gated_sem.at[step - 1, SIDE], recv_sem=gated_sem.at[step - 1, col_x],
                    device_id={"chan": at_x(i)}, device_id_type=MESH,
                ).start()
    for i in (1, 3, 2):
        source = lax.rem(col_x + i, SIDE)
        mine = weight_half(source, core)
        pltpu.make_async_copy(mine, mine, weight_sem.at[source]).wait()
        rows = pl.ds(pl.multiple_of(source * 2 * half_k + half_rows, half_k), half_k)
        for block in range(SIDE):
            pltpu.make_async_remote_copy(
                src_ref=weight.at[block, rows, :], dst_ref=weight.at[block, rows, :],
                send_sem=pair_sem.at[SIDE], recv_sem=pair_sem.at[source],
                device_id={"seq": sibling}, device_id_type=MESH,
            ).start()
    for i in range(SIDE):
        own_weight(i).wait()
    for i in (1, 3, 2):
        source = lax.rem(col_x + i, SIDE)
        other = weight_half(source, 1 - core)
        pltpu.make_async_copy(other, other, pair_sem.at[source]).wait()

    def pass_on(kind, step, way):
        pltpu.make_async_remote_copy(
            src_ref=part_send.at[kind, step, way], dst_ref=part_recv.at[kind, step, way],
            send_sem=part_sem.at[3, 0, 0], recv_sem=part_sem.at[kind, step, way],
            device_id={"chan": at_y(1 if way == 0 else 3)}, device_id_type=MESH,
        ).start()

    def arrived(kind, step, way):
        ref = part_recv.at[kind, step, way]
        pltpu.make_async_copy(ref, ref, part_sem.at[kind, step, way]).wait()
        return ref[...].astype(F32)

    half_cols = cols_each // 2
    for step in range(STEPS):
        for i in (1, 3, 2):
            part = gated_part(step, lax.rem(col_x + i, SIDE))
            pltpu.make_async_copy(part, part, gated_sem.at[step, lax.rem(col_x + i, SIDE)]).wait()
        rows = pl.ds(step * chunk, chunk)

        def block_half(away, half):
            target = lax.rem(col_y + away, SIDE)
            return dot(gated[rows, :], weight[target, :, pl.ds(half * half_cols, half_cols)])

        for way in range(2):
            part_send[FAR, step, way] = block_half(2, way).astype(BF16)
            pass_on(FAR, step, way)
        for way, away in ((0, 1), (1, 3)):
            part_send[DIRECT, step, way] = block_half(away, 1 - way).astype(BF16)
            pass_on(DIRECT, step, way)
        for way, away in ((0, 1), (1, 3)):
            kept[step, way] = block_half(away, way)
        for half in range(2):
            total[rows, pl.ds(half * half_cols, half_cols)] = block_half(0, half)
    for step in range(STEPS):
        for way in range(2):
            part_send[MERGED, step, way] = (kept[step, way] + arrived(FAR, step, way)).astype(BF16)
            pass_on(MERGED, step, way)
    for step in range(STEPS):
        rows = pl.ds(step * chunk, chunk)
        for way in range(2):
            total[rows, pl.ds((1 - way) * half_cols, half_cols)] += arrived(DIRECT, step, way)
    for step in range(STEPS):
        for way in range(2):
            cols = pl.ds(way * half_cols, half_cols)
            done = total[pl.ds(step * chunk, chunk), cols] + arrived(MERGED, step, way)
            for low in range(HALF // STEPS):
                for high in range(2):
                    piece = done[(low * 2 + high) * SPAN:(low * 2 + high + 1) * SPAN]
                    place = (high * HALF + step * (HALF // STEPS) + low) * SPAN
                    out[pl.ds(place, SPAN), cols] = piece.astype(BF16)
    settled(tok_send, send_sem.at[0])
    settled(spec_send, send_sem.at[1])
    settled(back_send, send_sem.at[2])
    three = weight.at[:, pl.ds(0, 3 * half_k), :]
    pltpu.make_async_copy(three, three, weight_sem.at[SIDE]).wait()
    pltpu.make_async_copy(three, three, pair_sem.at[SIDE]).wait()
    for step in range(STEPS):
        sent = gated.at[pl.ds(step * chunk, chunk), pl.ds(0, 3 * width)]
        pltpu.make_async_copy(sent, sent, gated_sem.at[step, SIDE]).wait()
    pltpu.make_async_copy(part_send, part_send, part_sem.at[3, 0, 0]).wait()


def layer(values, gate_in, gate_out, spectrum, out_weight):
    forward, inverse, twist, mix, unmix, pick, pick_t, fold = tables()
    rows, width = values.shape
    cols_each = out_weight.shape[1] // (SIDE * SIDE)
    flat = spectrum.reshape(2 * SPAN * SPAN, width)
    loaded = [(values.shape, BF16)] * 3 + [((2, 2 * SPAN * SPAN, LANES), F32)]
    loaded += [(t.shape, F32 if t.dtype == np.float32 else BF16) for t in
               (forward, inverse, twist, mix, unmix, pick, pick_t, fold)]
    scratch = [pltpu.VMEM(shape, dtype) for shape, dtype in loaded]
    scratch += [
        pltpu.VMEM((SEQ * HALF, LANES), F32),
        pltpu.VMEM((SEQ, HALF, LANES), BF16),
        pltpu.VMEM((SEQ, HALF, LANES), BF16),
        pltpu.VMEM((SEQ * SPAN, LANES), F32),
        pltpu.VMEM((SEQ, SPAN, LANES), BF16),
        pltpu.VMEM((SEQ, SPAN, LANES), BF16),
        pltpu.VMEM((BLOCK, 2 * LANES), F32),
        pltpu.VMEM((2 * BLOCK, LANES), BF16),
        pltpu.VMEM((SEQ, HALF, LANES), BF16),
        pltpu.VMEM((SEQ, HALF, LANES), BF16),
        pltpu.VMEM((SIDE, SIDE * width, cols_each), BF16),
        pltpu.VMEM((rows, SIDE * width), BF16),
        pltpu.VMEM((rows, cols_each), F32),
        pltpu.VMEM((STEPS, 2, rows // STEPS, cols_each // 2), F32),
        pltpu.VMEM((3, STEPS, 2, rows // STEPS, cols_each // 2), BF16),
        pltpu.VMEM((3, STEPS, 2, rows // STEPS, cols_each // 2), BF16),
        pltpu.SemaphoreType.DMA((len(loaded) + 1 + SIDE,)),
        pltpu.SemaphoreType.DMA((3,)),
        pltpu.SemaphoreType.DMA((3, 4)),
        pltpu.SemaphoreType.DMA((SIDE + 1,)),
        pltpu.SemaphoreType.DMA((SIDE + 1,)),
        pltpu.SemaphoreType.DMA((STEPS, SIDE + 1)),
        pltpu.SemaphoreType.DMA((4, STEPS, 2)),
    ]
    return pl.pallas_call(
        layer_kernel,
        out_shape=jax.ShapeDtypeStruct((rows, cols_each), BF16),
        in_specs=[pl.BlockSpec(memory_space=pltpu.HBM)] * 13,
        out_specs=pl.BlockSpec(memory_space=pltpu.VMEM),
        scratch_shapes=scratch,
        compiler_params=pltpu.CompilerParams(
            collective_id=0, has_side_effects=True, vmem_limit_bytes=32 << 20
        ),
        name="layer",
    )(*[
        pltpu.with_memory_space_constraint(t, pltpu.HBM)
        for t in (values, gate_in, gate_out, flat, out_weight)
    ], *[
        pltpu.with_memory_space_constraint(jnp.asarray(t), pltpu.HBM)
        for t in (forward, inverse, twist, mix, unmix, pick, pick_t, fold)
    ])


def solution(mesh):
    placed = (
        P("seq", "chan"),
        P("seq", "chan"),
        P("seq", "chan"),
        P(None, None, "seq", "chan"),
        P("chan", None),
    )
    return jax.shard_map(
        layer, mesh=mesh, in_specs=placed, out_specs=P("seq", "chan"), check_vma=False
    )
```
